256 devices in a mesh: expert: 64 (over z, y, core), slot: 4 (over x).
Axes of the slice: x: 4, y: 4, z: 8, core: 2. Of those that a mesh axis runs over, the one named last changes fastest.
Arguments:
- tokens: bfloat16 [32768, 2048], P(('expert', 'slot')), may hold values from -6 to 6
- out_grad: bfloat16 [32768, 2048], P(('expert', 'slot')), may hold values from -6 to 6
- routing: int32 [32768, 1], P(('expert', 'slot')), may hold values from 0 to 63; in each aligned block of 128 rows (0 to 127, 128 to 255, ...) at most 4 rows name the same one
- plan: int32 [64], replicated, may hold values from 0 to 47, as said below
- gate_weight: bfloat16 [64, 2048, 768], P('expert', None, 'slot'), as said below
- up_weight: bfloat16 [64, 2048, 768], P('expert', None, 'slot'), as said below
- down_weight: bfloat16 [64, 768, 2048], P('expert', 'slot'), as said below
- master: float32 [48, 768, 2048], P(None, ('slot', 'expert'))
- moment: float32 [48, 768, 2048], P(None, ('slot', 'expert')), may hold values from -24 to 24
- second: float32 [48, 768, 2048], P(None, ('slot', 'expert')), may hold values from 1 to 400
Outputs:
- token_grad: bfloat16 [32768, 2048], P(('expert', 'slot'))
- new_master: float32 [48, 768, 2048], P(None, ('slot', 'expert'))
- new_moment: float32 [48, 768, 2048], P(None, ('slot', 'expert'))
- new_second: float32 [48, 768, 2048], P(None, ('slot', 'expert'))
- new_down: bfloat16 [64, 768, 2048], P('expert', 'slot')
The draws below stay inside these ranges and needn't reach their ends.
Inputs may be any that keep to these rules, and one draw needn't show every extreme that they name: `routing`: in the rows of one device no slot is named more than 4 times, a bound that some block reaches. `plan`: every expert 0 to 47 is held by at least one slot. `gate_weight`: slots holding the same expert have equal gate and up projections. `up_weight`: slots holding the same expert have equal gate and up projections. down_weight[k] is master[plan[k]] rounded to bfloat16.
All inputs are finite; a program needn't handle non-finite values.
Results may differ from the reference program's by a relative error of at most 0.012.
Values may be sent and summed in bfloat16 or wider, within the bound.
A program may use at most 128 MiB of HBM per device.

```python
import math
import jax
import jax.numpy as jnp
import numpy as np
from jax import lax

D = 2048
FF = 768
TOK_DEV = 128
SLOTS = 64
PRIM = 48
CAP = 4
TOKENS = 32768
N_EXPERT = 64
N_SLOT = 4


def plan_from(key):
    base_key = jax.random.fold_in(key, 11)
    order = jax.random.permutation(jax.random.fold_in(base_key, 1), SLOTS)
    extra = jax.random.randint(jax.random.fold_in(base_key, 2), (SLOTS - PRIM,), 0, PRIM)
    listed = jnp.concatenate((jnp.arange(PRIM, dtype=jnp.int32), extra.astype(jnp.int32)))
    return listed[order].astype(jnp.int32)


def master_from(key):
    values = jax.random.normal(jax.random.fold_in(key, 21), (PRIM, FF, D), jnp.float32)
    return values * FF ** (-0.5)


def draw_plan(key, part):
    return plan_from(key)


def draw_master(key, part):
    return master_from(key)


def draw_down_weight(key, part):
    return master_from(key)[plan_from(key)].astype(jnp.bfloat16)


def draw_gate_weight(key, part):
    values = jax.random.normal(jax.random.fold_in(key, 31), (PRIM, D, FF), jnp.float32) * D ** (-0.5)
    return values[plan_from(key)].astype(jnp.bfloat16)


def draw_up_weight(key, part):
    values = jax.random.normal(jax.random.fold_in(key, 32), (PRIM, D, FF), jnp.float32) * D ** (-0.5)
    return values[plan_from(key)].astype(jnp.bfloat16)


def level_of(rng, extent, shards, smallest, largest):
    def one(dim, parts):
        steps = jax.random.uniform(jax.random.fold_in(jax.random.fold_in(rng, 6), dim), (parts,), jnp.float32, smallest / len(shards), largest / len(shards))
        return jnp.repeat(jnp.exp(steps), extent[dim] // parts).reshape((-1,) + (1,) * (len(extent) - dim - 1))

    gain = one(*shards[0])
    for cut in shards[1:]:
        gain = gain * one(*cut)
    return gain


def assign_block(own_key, own, number, rows, number_of, top, most, lean):
    order = jax.random.permutation(own_key, number_of)
    heavy_load, common = portions_of(number_of, rows * top, most, lean, True), portions_of(number_of, rows * top, most, lean, False)
    places = jnp.arange(number_of)

    def named(sizes, offset_by):
        used = int((sizes > 0).sum())
        fixed = max(1, used // 4)
        shifted = fixed + (places - fixed + offset_by * (used - fixed)) % max(1, number_of - fixed)
        return jnp.zeros((number_of,), jnp.int32).at[order[jnp.where(places < fixed, places, shifted)]].set(jnp.asarray(sizes, jnp.int32))

    sizes = jnp.where(number % 4 == 0, named(heavy_load, number // 4), named(common, number - number // 4 - 1))
    mixed = jax.random.permutation(jax.random.fold_in(own, 3), number_of)
    giver, receiver = mixed[0:number_of // 2 * 2:2], mixed[1:number_of // 2 * 2:2]
    margin = jnp.minimum(sizes[giver] - 1, most - sizes[receiver]) // 2
    margin = jnp.where((giver == order[0]) | (receiver == order[0]) | (sizes[receiver] == 0), 0, jnp.maximum(margin, 0))
    shifted = jax.random.randint(jax.random.fold_in(own, 4), (number_of // 2,), 0, 1 << 20) % (margin + 1)
    sizes = sizes.at[giver].add(-shifted).at[receiver].add(shifted)
    labels = jnp.searchsorted(jnp.cumsum(sizes), jnp.arange(rows * top), side="right").astype(jnp.int32)
    grid = labels.reshape(top, rows).T
    grid = grid[jax.random.permutation(jax.random.fold_in(own, 1), rows)]
    offset_by = jax.random.randint(jax.random.fold_in(own, 2), (rows, 1), 0, top)
    return jnp.take_along_axis(grid, (jnp.arange(top)[None, :] + offset_by) % top, axis=1)


def portions_of(amount, total, most, lean, full):
    loads = [(1 << 20) // math.isqrt(standing ** lean) + 1 for standing in range(1, amount + 1)]
    largest = most if full else min(most, max(-(-total // amount), total * loads[0] // sum(loads)))
    least = 1 if total - largest >= amount - 1 else 0
    given, spare = [largest] + [least] * (amount - 1), total - largest - least * (amount - 1)
    while spare > 0:
        candidates = [i for i in range(1, amount) if given[i] < largest] or [i for i in range(1, amount) if given[i] < most]
        mass, remaining = sum([loads[i] for i in candidates]), spare
        for i in candidates:
            more = min(most - given[i], max(1, remaining * loads[i] // mass), spare)
            given[i] = given[i] + more
            spare = spare - more
    return np.array(given)


def centred(own_key, dims, spread, most, pieces=(), kind=jnp.bfloat16):
    entries = spread * jax.random.normal(own_key, dims, jnp.float32)
    if pieces:
        entries = entries * level_of(own_key, dims, pieces, -0.22, 0.18)
    return jnp.clip(entries, -most, most).astype(kind)


def setup_inputs(seed: int = 0) -> dict:
    arg_keys = jax.random.split(jax.random.key(seed), 11)
    tokens = centred(arg_keys[0], (TOKENS, D), 1.0, 6.0, ((0, 256),))
    out_grad = centred(arg_keys[1], (TOKENS, D), 1.0, 6.0, ((0, 256),))
    routing_keys = jax.random.split(jax.random.fold_in(arg_keys[2], 1), TOKENS // TOK_DEV)
    routing_turns = jax.random.permutation(jax.random.fold_in(arg_keys[2], 3), TOKENS // TOK_DEV)
    routing = jax.vmap(lambda own, number: assign_block(jax.random.fold_in(arg_keys[2], 2), own, number, TOK_DEV, SLOTS, 1, CAP, 2))(routing_keys, routing_turns).reshape((TOKENS, 1))
    plan = draw_plan(jax.random.fold_in(arg_keys[10], 71), 0)
    gate_weight = draw_gate_weight(jax.random.fold_in(arg_keys[10], 71), 0)
    up_weight = draw_up_weight(jax.random.fold_in(arg_keys[10], 71), 0)
    down_weight = draw_down_weight(jax.random.fold_in(arg_keys[10], 71), 0)
    master = draw_master(jax.random.fold_in(arg_keys[10], 71), 0)
    moment = centred(arg_keys[8], (PRIM, FF, D), 4.0, 24.0, ((1, 256),), jnp.float32)
    second = jnp.clip(jnp.exp(math.log(400.0) - 5.9914645 * jax.random.uniform(arg_keys[9], (PRIM, FF, D), jnp.float32) ** level_of(arg_keys[9], (PRIM, FF, D), ((1, 256),), -0.2, 0.2)), 1.0, 400.0)
    return dict(tokens=tokens, out_grad=out_grad, routing=routing, plan=plan, gate_weight=gate_weight, up_weight=up_weight, down_weight=down_weight, master=master, moment=moment, second=second)


def adam_update(folded, master, moment, second):
    new_moment = 0.9 * moment + 0.1 * folded
    new_second = 0.95 * second + 0.05 * folded * folded
    first_hat = new_moment / (1.0 - 0.9 ** 10)
    second_hat = new_second / (1.0 - 0.95 ** 10)
    new_master = master - 0.01 * (first_hat / (jnp.sqrt(second_hat) + 1e-08) + 0.1 * master)
    return (new_master, new_moment, new_second)

def reference(tokens, out_grad, routing, plan, gate_weight, up_weight, down_weight, master, moment, second):
    sources = N_EXPERT * N_SLOT
    route = routing[:, 0].reshape(sources, TOK_DEV)
    onehot = (route[:, :, None] == jnp.arange(SLOTS, dtype=jnp.int32)[None, None, :]).astype(jnp.int32)
    rank = lax.optimization_barrier(jnp.sum(jnp.cumsum(onehot, axis=1) * onehot, axis=2)) - 1
    anchor = jnp.arange(sources, dtype=jnp.int32)[:, None]
    position = (route * (sources * CAP) + anchor * CAP + rank).reshape(-1).astype(jnp.int32)
    total = SLOTS * sources * CAP
    x_buffer = jnp.zeros((total, D), jnp.bfloat16).at[position].set(tokens).reshape(SLOTS, sources * CAP, D)
    g_buffer = jnp.zeros((total, D), jnp.bfloat16).at[position].set(out_grad).reshape(SLOTS, sources * CAP, D)

    def one_slot(items):
        x_rows, g_rows, w_gate, w_up, w_down = items
        gate = jnp.dot(x_rows, w_gate, preferred_element_type=jnp.float32)
        up = jnp.dot(x_rows, w_up, preferred_element_type=jnp.float32)
        sig = jax.nn.sigmoid(gate)
        silu_gate = gate * sig
        hidden = (silu_gate * up).astype(jnp.bfloat16)
        d_hidden = jnp.dot(g_rows, w_down.T, preferred_element_type=jnp.float32)
        d_gate = (d_hidden * up * sig * (1.0 + gate * (1.0 - sig))).astype(jnp.bfloat16)
        d_up = (d_hidden * silu_gate).astype(jnp.bfloat16)
        d_input = jnp.dot(d_gate, w_gate.T, preferred_element_type=jnp.float32)
        d_input = d_input + jnp.dot(d_up, w_up.T, preferred_element_type=jnp.float32)
        grad = jnp.dot(hidden.T, g_rows, preferred_element_type=jnp.float32)
        return (d_input.astype(jnp.bfloat16), grad)
    dx_buffer, grads = lax.map(one_slot, (x_buffer, g_buffer, gate_weight, up_weight, down_weight))
    token_grad = dx_buffer.reshape(total, D)[position]
    select = (plan[None, :] == jnp.arange(PRIM, dtype=jnp.int32)[:, None]).astype(jnp.float32)
    folded = jnp.einsum('ps,sfd->pfd', select, grads, precision=lax.Precision.HIGHEST)
    new_master, new_moment, new_second = adam_update(folded, master, moment, second)
    new_down = new_master.astype(jnp.bfloat16)[plan]
    return (token_grad, new_master, new_moment, new_second, new_down)
```

```python
import functools

import jax
import jax.numpy as jnp
from jax import lax
from jax.experimental import pallas as pl
from jax.experimental.pallas import tpu as pltpu
from jax.sharding import PartitionSpec as P

MESH = pl.DeviceIdType.MESH
BF = jnp.bfloat16
F32 = jnp.float32


def dot(a, b, ca, cb):
    return lax.dot_general(a, b, (((ca,), (cb,)), ((), ())), preferred_element_type=F32)


def one(mask):
    return jnp.where(mask, 1.0, 0.0).astype(BF)


def iota(shape, dim):
    return lax.broadcasted_iota(jnp.int32, shape, dim)


def offset(i):
    return 4 + (i // 2) * (1 - 2 * (i % 2)) - (i % 2)


def kernel(
    tok, og, route, plan, gw, uw, dw, mst, mom, sec,
    tg, nms, nmo, nse, nd,
    dense, routes, pos, sx, rows, w, hid, dg, du, hidt,
    dxs, dxr, dxo, rets, retr, tgv,
    gsend, gpart, gown, vst, gs, grecv, planv, mt, states, news, nmb, nds, ndr, ndo,
    load_sem, swap_s, swap_r, disp_s, disp_r, fwd_s, fwd_r, wt_s, wt_r,
    dx_s, dx_r, ret_s, ret_r, tg_s, tg_r, gp_s, gp_r, ga_s, ga_r, nd_s, nd_r, out_sem,
):
    me = lax.axis_index("expert")
    s = lax.axis_index("slot")
    core = me % 2
    chip = me // 2
    z = chip // 4
    y = chip % 4
    other = me + 1 - 2 * core
    tpart = s + 1 - 2 * (s % 2)
    wpart = (s + 1 + 2 * ((s + 1) % 2)) % 4

    def remote(src, dst, ss, rs, e, x):
        return pltpu.make_async_remote_copy(
            src_ref=src, dst_ref=dst, send_sem=ss, recv_sem=rs, device_id=(e, x), device_id_type=MESH
        )

    def local(src, dst, sem):
        return pltpu.make_async_copy(src, dst, sem)

    @pl.when(core == 0)
    def _():
        local(tok, dense.at[core], load_sem.at[0]).start()

    @pl.when(core == 1)
    def _():
        local(og, dense.at[core], load_sem.at[0]).start()

    local(route, routes.at[core], load_sem.at[1]).start()
    local(plan, planv, load_sem.at[2]).start()
    for k, src in enumerate((gw, uw, dw)):
        local(src, w.at[k, pl.ds(0, 192)], load_sem.at[3 + k]).start()
    for k, src in enumerate((mst, mom, sec)):
        local(src, states.at[k], load_sem.at[6 + k]).start()

    barrier = pltpu.get_barrier_semaphore()

    @pl.loop(1, 64)
    def _(k):
        pl.semaphore_signal(barrier, inc=1, device_id=((me + k) % 64, s), device_id_type=MESH)

    for x in (tpart, wpart):
        pl.semaphore_signal(barrier, inc=1, device_id=(me, x), device_id_type=MESH)
    pl.semaphore_wait(barrier, 65)

    @pl.when(core == 0)
    def _():
        remote(og, dense.at[core], swap_s.at[0], swap_r.at[0], other, s).start()

    @pl.when(core == 1)
    def _():
        remote(tok, dense.at[core], swap_s.at[0], swap_r.at[0], other, s).start()

    remote(route, routes.at[core], swap_s.at[1], swap_r.at[1], other, s).start()
    for k, src in enumerate((gw, uw, dw)):
        remote(src, w.at[k, pl.ds(192, 192)], wt_s.at[k], wt_r.at[k], me, wpart).start()

    local(route, routes.at[core], load_sem.at[1]).wait()
    remote(route, routes.at[core], swap_s.at[1], swap_r.at[1], other, s).wait()
    upper = one(iota((128, 128), 0) < iota((128, 128), 1))
    for c in range(2):
        hit = iota((64, 128), 0) == routes[c]
        before = dot(one(hit), upper, 1, 0)
        rank = jnp.sum(jnp.where(hit, before, 0.0), axis=0, keepdims=True)
        pos[:, c * 128 : (c + 1) * 128] = routes[c].astype(F32) * 8.0 + (c * 4.0) + rank

    local(tok, dense.at[core], load_sem.at[0]).wait()
    remote(tok, dense.at[core], swap_s.at[0], swap_r.at[0], other, s).wait()

    def dispatch(i, carry):
        zt = (z + offset(i)) % 8
        pick = one((iota((64, 256), 0) + zt * 64).astype(F32) == pos[...])
        block = dot(pick, dense[...].reshape(256, 2048), 1, 0).astype(BF)
        sx[pl.ds(zt * 8, 8)] = block.reshape(8, 8, 2048)
        for dy in (2, 1, 3, 0):
            for dc in (1, 0):
                e = (zt * 4 + (y + dy) % 4) * 2 + (core + dc) % 2
                dst = rows.at[core, 0, i * 4 + y]

                def send():
                    remote(sx.at[e], dst, disp_s, disp_r.at[i], e, s).start()

                if dy == 0 and dc == 0:
                    @pl.when(i == 7)
                    def _():
                        local(sx.at[e], dst, disp_r.at[i]).start()

                    pl.when(i != 7)(send)
                else:
                    send()
        return carry

    lax.fori_loop(0, 8, dispatch, 0)

    def group(who, i):
        return rows.at[:, who, pl.ds(i * 4, 4)]

    def forward(i, carry):
        local(group(0, i), group(0, i), disp_r.at[i]).wait()
        remote(group(0, i), group(1, i), fwd_s.at[i], fwd_r.at[i], me, tpart).start()
        return carry

    lax.fori_loop(0, 8, forward, 0)

    for k, src in enumerate((gw, uw, dw)):
        local(src, w.at[k, pl.ds(0, 192)], load_sem.at[3 + k]).wait()
        remote(src, w.at[k, pl.ds(192, 192)], wt_s.at[k], wt_r.at[k], me, wpart).wait()

    def first(q, carry):
        who = q % 2
        half = q // 2

        @pl.when(who == 1)
        def _():
            for d in range(4):
                i = half * 4 + d
                remote(group(0, i), group(1, i), fwd_s.at[i], fwd_r.at[i], me, tpart).wait()

        x = rows[0, who, pl.ds(half * 16, 16)].reshape(128, 2048)
        g = rows[1, who, pl.ds(half * 16, 16)].reshape(128, 2048)
        gate = dot(x, w[0], 1, 1)
        up = dot(x, w[1], 1, 1)
        dh = dot(g, w[2], 1, 1)
        sig = jax.nn.sigmoid(gate)
        silu = gate * sig
        at = pl.ds(pl.multiple_of(half * 128, 128), 128)
        hid[who, at, :] = (silu * up).astype(BF)
        dg[who, at, :] = (dh * up * sig * (1.0 + gate * (1.0 - sig))).astype(BF)
        du[who, at, :] = (dh * silu).astype(BF)
        return carry

    lax.fori_loop(0, 4, first, 0)

    def columns(n, size):
        return pl.ds(pl.multiple_of(n * size, size), size)

    def partial(who, n):
        c = columns(n, 512)
        return dot(dg[who], w[0, :, c], 1, 0) + dot(du[who], w[1, :, c], 1, 0)

    def dx_copy(n):
        c = columns(n, 512)
        return remote(dxs.at[:, :, c], dxr.at[:, :, c], dx_s.at[n], dx_r.at[n], me, tpart)

    def send_partial(n, carry):
        dxs[:, :, columns(n, 512)] = partial(1, n).astype(BF).reshape(32, 8, 512)
        dx_copy(n).start()
        return carry

    lax.fori_loop(0, 4, send_partial, 0)

    u = iota((384, 384), 0)
    v = iota((384, 384), 1)
    turn = one((u // 192 == v // 192) & (u % 192 == (v % 64) * 3 + (v % 192) // 64))
    for who in range(2):
        hidt[:, who * 256 : (who + 1) * 256] = dot(turn, hid[who], 0, 1).astype(BF)

    def gsum(lo, n):
        c = columns(n, 512)
        out = dot(hidt[lo : lo + 192, 0:256], rows[1, 0, :, :, c].reshape(256, 512), 1, 0)
        return out + dot(hidt[lo : lo + 192, 256:512], rows[1, 1, :, :, c].reshape(256, 512), 1, 0)

    def gp_copy(n):
        c = columns(n, 512)
        return remote(gsend.at[:, c], gpart.at[:, c], gp_s.at[n], gp_r.at[n], me, wpart)

    def send_grad(n, carry):
        gsend[:, columns(n, 512)] = gsum(192, n).astype(BF)
        gp_copy(n).start()
        return carry

    lax.fori_loop(0, 4, send_grad, 0)

    def own(n, carry):
        dxo[:, columns(n, 512)] = partial(0, n)
        gown[:, columns(n, 512)] = gsum(0, n)
        return carry

    lax.fori_loop(0, 4, own, 0)

    for h in range(2):
        for n in (2 * h, 2 * h + 1):
            dx_copy(n).wait()
            c = slice(n * 512, (n + 1) * 512)
            total = dxo[:, c] + dxr[:, :, c].reshape(256, 512).astype(F32)
            rets[:, :, c] = total.astype(BF).reshape(32, 8, 512)

        def give(q, carry):
            i = q // 4
            yy = q % 4
            e = (((z + 8 - offset(i)) % 8) * 4 + yy) * 2 + h
            src = rets.at[q, :, h * 1024 : (h + 1) * 1024]

            @pl.when(e == me)
            def _():
                local(src, retr.at[me], ret_r).start()

            @pl.when(e != me)
            def _():
                remote(src, retr.at[me], ret_s, ret_r, e, s).start()

            return carry

        lax.fori_loop(0, 32, give, 0)

    local(plan, planv, load_sem.at[2]).wait()
    spread = one(iota((64, 512), 0) == iota((64, 512), 1) // 8)
    held = dot(planv[...].astype(F32).astype(BF), spread, 1, 0)
    r = iota((384, 512), 0)
    mt[...] = one((r // 48 == iota((384, 512), 1) % 8) & ((r % 48).astype(F32) == held))

    for n in range(4):
        gp_copy(n).wait()
        for b in (2 * n, 2 * n + 1):
            c = slice(b * 256, (b + 1) * 256)
            total = (gown[:, c] + gpart[:, c].astype(F32)).astype(BF)
            for j in range(3):
                vst[b * 64 : (b + 1) * 64, j * 256 : (j + 1) * 256] = total[j * 64 : (j + 1) * 64]
    a = iota((512, 512), 0)
    d = iota((512, 512), 1)
    weave = one((a // 8 == d % 64) & (a % 8 == d // 64))
    gs[...] = dot(weave, vst[...], 1, 0).astype(BF).reshape(64, 8, 768)

    def exchange(src, dst, ss, rs):
        def go(k, carry):
            zt = (z + offset(k // 8)) % 8
            e = (zt * 4 + (y + k // 2) % 4) * 2 + (core + k) % 2

            @pl.when(e == me)
            def _():
                local(src.at[e], dst.at[me], rs).start()

            @pl.when(e != me)
            def _():
                remote(src.at[e], dst.at[me], ss, rs, e, s).start()

            return carry

        lax.fori_loop(0, 64, go, 0)

    exchange(gs, grecv, ga_s, ga_r)

    local(retr, retr, ret_r).wait()
    place = one(iota((512, 256), 0).astype(F32) == pos[...])
    for n in range(2):
        c = slice(n * 512, (n + 1) * 512)
        tgv[:, :, c] = dot(place, retr[:, :, c].reshape(512, 512), 0, 0).astype(BF).reshape(2, 128, 512)
    mine = pl.ds(pl.multiple_of(core * 1024, 1024), 1024)
    tg_local = local(tgv.at[core], tg.at[:, mine], out_sem.at[0])
    tg_remote = remote(tgv.at[1 - core], tg.at[:, mine], tg_s, tg_r, other, s)
    tg_local.start()
    tg_remote.start()

    for k, src in enumerate((mst, mom, sec)):
        local(src, states.at[k], load_sem.at[6 + k]).wait()
    local(grecv, grecv, ga_r).wait()

    def update(b, carry):
        at = pl.ds(pl.multiple_of(b * 48, 48), 48)
        c = columns(b, 256)
        fold = dot(mt[at, :], grecv[...].reshape(512, 768), 1, 0)
        for j in range(3):
            f = fold[:, j * 256 : (j + 1) * 256]
            m0 = states[0, j, :, c]
            nm = 0.9 * states[1, j, :, c] + 0.1 * f
            ns = 0.95 * states[2, j, :, c] + 0.05 * f * f
            first_hat = nm / (1.0 - 0.9**10)
            second_hat = ns / (1.0 - 0.95**10)
            new = m0 - 0.01 * (first_hat / (jnp.sqrt(second_hat) + 1e-08) + 0.1 * m0)
            news[0, j, :, c] = new
            news[1, j, :, c] = nm
            news[2, j, :, c] = ns
            nmb[at, j * 256 : (j + 1) * 256] = new.astype(BF)
        return carry

    lax.fori_loop(0, 8, update, 0)
    nds[...] = dot(mt[...], nmb[...], 0, 0).astype(BF).reshape(64, 8, 768)
    exchange(nds, ndr, nd_s, nd_r)
    for k, dst in enumerate((nms, nmo, nse)):
        local(news.at[k], dst, out_sem.at[1 + k]).start()

    local(ndr, ndr, nd_r).wait()
    vst[...] = dot(weave, ndr[...].reshape(512, 768), 0, 0).astype(BF)
    turn_back = one(iota((192, 192), 0) == (iota((192, 192), 1) % 64) * 3 + iota((192, 192), 1) // 64)
    for b in range(8):
        stack = [vst[b * 64 : (b + 1) * 64, j * 256 : (j + 1) * 256] for j in range(3)]
        ndo[:, b * 256 : (b + 1) * 256] = dot(turn_back, jnp.concatenate(stack, axis=0), 1, 0).astype(BF)
    last = local(ndo, nd, out_sem.at[4])
    last.start()

    for k, dst in enumerate((nms, nmo, nse)):
        local(news.at[k], dst, out_sem.at[1 + k]).wait()
    tg_local.wait()
    tg_remote.wait()
    remote(sx.at[pl.ds(0, 63)], sx.at[pl.ds(0, 63)], disp_s, disp_s, other, s).wait_send()
    remote(retr.at[pl.ds(0, 63)], retr.at[pl.ds(0, 63)], ret_s, ret_s, other, s).wait_send()
    remote(gs.at[pl.ds(0, 63)], gs.at[pl.ds(0, 63)], ga_s, ga_s, other, s).wait_send()
    remote(nds.at[pl.ds(0, 63)], nds.at[pl.ds(0, 63)], nd_s, nd_s, other, s).wait_send()
    last.wait()


def body(tokens, out_grad, routing, plan, gate_weight, up_weight, down_weight, master, moment, second):
    any_ = pl.BlockSpec(memory_space=pl.ANY)
    vm = pltpu.VMEM
    dma = pltpu.SemaphoreType.DMA
    outs = pl.pallas_call(
        kernel,
        out_shape=(
            jax.ShapeDtypeStruct((128, 2048), BF),
            jax.ShapeDtypeStruct((3, 48, 2048), F32),
            jax.ShapeDtypeStruct((3, 48, 2048), F32),
            jax.ShapeDtypeStruct((3, 48, 2048), F32),
            jax.ShapeDtypeStruct((192, 2048), BF),
        ),
        in_specs=[any_] * 10,
        out_specs=[any_] * 5,
        scratch_shapes=[
            vm((2, 128, 2048), BF),
            vm((2, 1, 128), jnp.int32),
            vm((1, 256), F32),
            vm((64, 8, 2048), BF),
            vm((2, 2, 32, 8, 2048), BF),
            vm((3, 384, 2048), BF),
            vm((2, 256, 384), BF),
            vm((2, 256, 384), BF),
            vm((2, 256, 384), BF),
            vm((384, 512), BF),
            vm((32, 8, 2048), BF),
            vm((32, 8, 2048), BF),
            vm((256, 2048), F32),
            vm((32, 8, 2048), BF),
            vm((64, 8, 1024), BF),
            vm((2, 128, 1024), BF),
            vm((192, 2048), BF),
            vm((192, 2048), BF),
            vm((192, 2048), F32),
            vm((512, 768), BF),
            vm((64, 8, 768), BF),
            vm((64, 8, 768), BF),
            vm((1, 64), jnp.int32),
            vm((384, 512), BF),
            vm((3, 3, 48, 2048), F32),
            vm((3, 3, 48, 2048), F32),
            vm((384, 768), BF),
            vm((64, 8, 768), BF),
            vm((64, 8, 768), BF),
            vm((192, 2048), BF),
            dma((9,)),
            dma((2,)), dma((2,)),
            dma, dma((8,)),
            dma((8,)), dma((8,)),
            dma((3,)), dma((3,)),
            dma((4,)), dma((4,)),
            dma, dma,
            dma, dma,
            dma((4,)), dma((4,)),
            dma, dma,
            dma, dma,
            dma((5,)),
        ],
        compiler_params=pltpu.CompilerParams(
            collective_id=0, has_side_effects=True, vmem_limit_bytes=60 * 1024 * 1024
        ),
    )(
        tokens,
        out_grad,
        routing.reshape(1, 128),
        plan.reshape(1, 64),
        jnp.transpose(gate_weight[0]),
        jnp.transpose(up_weight[0]),
        down_weight[0],
        jnp.transpose(master, (1, 0, 2)),
        jnp.transpose(moment, (1, 0, 2)),
        jnp.transpose(second, (1, 0, 2)),
    )
    token_grad, new_master, new_moment, new_second, new_down = outs
    back = lambda t: jnp.transpose(t, (1, 0, 2))
    return token_grad, back(new_master), back(new_moment), back(new_second), new_down[None]


def solution(mesh):
    placed = (
        P(("expert", "slot"), None),
        P(("expert", "slot"), None),
        P(("expert", "slot"), None),
        P(),
        P("expert", None, "slot"),
        P("expert", None, "slot"),
        P("expert", "slot", None),
        P(None, ("slot", "expert"), None),
        P(None, ("slot", "expert"), None),
        P(None, ("slot", "expert"), None),
    )
    return jax.shard_map(
        body,
        mesh=mesh,
        in_specs=placed,
        out_specs=(
            P(("expert", "slot"), None),
            P(None, ("slot", "expert"), None),
            P(None, ("slot", "expert"), None),
            P(None, ("slot", "expert"), None),
            P("expert", "slot", None),
        ),
        check_vma=False,
    )
```

```python
import functools

import jax
import jax.numpy as jnp
from jax import lax
from jax.experimental import pallas as pl
from jax.experimental.pallas import tpu as pltpu
from jax.sharding import PartitionSpec as P

MESH = pl.DeviceIdType.MESH
BF = jnp.bfloat16
F32 = jnp.float32


def dot(a, b, ca, cb):
    return lax.dot_general(a, b, (((ca,), (cb,)), ((), ())), preferred_element_type=F32)


def one(mask):
    return jnp.where(mask, 1.0, 0.0).astype(BF)


def iota(shape, dim):
    return lax.broadcasted_iota(jnp.int32, shape, dim)


def offset(i):
    h = i // 4
    j = (i + 3) % 4
    k = (i + 2) % 4
    near = 2 * ((j + 1) // 2) * (1 - 2 * (j % 2))
    far = (2 * (k // 2) + 1) * (2 * (k % 2) - 1)
    return 4 + (1 - h) * near + h * far


def kernel(
    tok, og, route, plan, gw, uw, dw, mst, mom, sec,
    tg, nms, nmo, nse, nd,
    dense, routes, pos, sx, rows, w, hid, dg, du, hidt,
    dxs, dxr, dxo, rets, retr, tgv,
    gsend, gpart, gown, vst, gs, grecv, planv, mt, states, news, nmb, nds, ndr, ndo,
    load_sem, swap_s, swap_r, disp_s, disp_r, fwd_s, fwd_r, wt_s, wt_r,
    dx_s, dx_r, ret_s, ret_r, tg_s, tg_r, gp_s, gp_r, ga_s, ga_r, nd_s, nd_r, out_sem,
):
    me = lax.axis_index("expert")
    s = lax.axis_index("slot")
    core = me % 2
    chip = me // 2
    z = chip // 4
    y = chip % 4
    other = me + 1 - 2 * core
    low = s + 1 - 2 * (s % 2)
    high = (s + 1 + 2 * ((s + 1) % 2)) % 4
    tpart = low + core * (high - low)
    wpart = high + core * (low - high)

    def remote(src, dst, ss, rs, e, x):
        return pltpu.make_async_remote_copy(
            src_ref=src, dst_ref=dst, send_sem=ss, recv_sem=rs, device_id=(e, x), device_id_type=MESH
        )

    def local(src, dst, sem):
        return pltpu.make_async_copy(src, dst, sem)

    @pl.when(core == 0)
    def _():
        local(tok, dense.at[core], load_sem.at[0]).start()

    @pl.when(core == 1)
    def _():
        local(og, dense.at[core], load_sem.at[0]).start()

    local(route, routes.at[core], load_sem.at[1]).start()
    local(plan, planv, load_sem.at[2]).start()
    for k, src in enumerate((gw, uw, dw)):
        local(src, w.at[k, pl.ds(0, 192)], load_sem.at[3 + k]).start()
    for k, src in enumerate((mst, mom, sec)):
        local(src, states.at[k], load_sem.at[6 + k]).start()

    barrier = pltpu.get_barrier_semaphore()

    @pl.loop(1, 64)
    def _(k):
        pl.semaphore_signal(barrier, inc=1, device_id=((me + k) % 64, s), device_id_type=MESH)

    for x in (tpart, wpart):
        pl.semaphore_signal(barrier, inc=1, device_id=(me, x), device_id_type=MESH)
    pl.semaphore_wait(barrier, 65)

    @pl.when(core == 0)
    def _():
        remote(og, dense.at[core], swap_s.at[0], swap_r.at[0], other, s).start()

    @pl.when(core == 1)
    def _():
        remote(tok, dense.at[core], swap_s.at[0], swap_r.at[0], other, s).start()

    remote(route, routes.at[core], swap_s.at[1], swap_r.at[1], other, s).start()
    for k, src in enumerate((gw, uw, dw)):
        remote(src, w.at[k, pl.ds(192, 192)], wt_s.at[k], wt_r.at[k], me, wpart).start()

    local(route, routes.at[core], load_sem.at[1]).wait()
    remote(route, routes.at[core], swap_s.at[1], swap_r.at[1], other, s).wait()
    upper = one(iota((128, 128), 0) < iota((128, 128), 1))
    for c in range(2):
        hit = iota((64, 128), 0) == routes[c]
        before = dot(one(hit), upper, 1, 0)
        rank = jnp.sum(jnp.where(hit, before, 0.0), axis=0, keepdims=True)
        pos[:, c * 128 : (c + 1) * 128] = routes[c].astype(F32) * 8.0 + (c * 4.0) + rank

    local(tok, dense.at[core], load_sem.at[0]).wait()
    remote(tok, dense.at[core], swap_s.at[0], swap_r.at[0], other, s).wait()

    def dispatch(i, carry):
        zt = (z + offset(i)) % 8
        pick = one((iota((64, 256), 0) + zt * 64).astype(F32) == pos[...])
        block = dot(pick, dense[...].reshape(256, 2048), 1, 0).astype(BF)
        sx[pl.ds(zt * 8, 8)] = block.reshape(8, 8, 2048)
        q = i * 4 + y
        dst = rows.at[core, 0, q]
        for dy in (2, 1, 0, 3):
            for dc in (1, 0):
                e = (zt * 4 + (y + dy) % 4) * 2 + (core + dc) % 2

                def send():
                    remote(sx.at[e], dst, disp_s, disp_r.at[q], e, s).start()

                if dy == 0 and dc == 0:
                    @pl.when(i == 0)
                    def _():
                        local(sx.at[e], dst, disp_r.at[q]).start()

                    pl.when(i != 0)(send)
                else:
                    send()
        return carry

    lax.fori_loop(0, 8, dispatch, 0)

    def span(who, q, n):
        return rows.at[:, who, pl.ds(q, n)]

    def forward(lo, hi):
        def go(k, carry):
            i = k // 4
            d = k % 4
            q = i * 4 + (y + 4 - (6 - 5 * d + 4 * (d // 2)) % 4) % 4
            local(span(0, q, 1), span(0, q, 1), disp_r.at[q]).wait()
            remote(span(0, q, 1), span(1, q, 1), fwd_s, fwd_r.at[i // 4], me, tpart).start()
            return carry

        lax.fori_loop(lo * 4, hi * 4, go, 0)

    def columns(n, size):
        return pl.ds(pl.multiple_of(n * size, size), size)

    def first(who, half):
        x = rows[0, who, half * 16 : half * 16 + 16].reshape(128, 2048)
        g = rows[1, who, half * 16 : half * 16 + 16].reshape(128, 2048)
        gate = dot(x, w[0], 1, 1)
        up = dot(x, w[1], 1, 1)
        dh = dot(g, w[2], 1, 1)
        sig = jax.nn.sigmoid(gate)
        silu = gate * sig
        at = slice(half * 128, half * 128 + 128)
        hid[who, at, :] = (silu * up).astype(BF)
        dg[who, at, :] = (dh * up * sig * (1.0 + gate * (1.0 - sig))).astype(BF)
        du[who, at, :] = (dh * silu).astype(BF)

    def wait_forward(half):
        remote(span(0, 0, 16), span(1, half * 16, 16), fwd_s, fwd_r.at[half], me, tpart).wait_recv()

    def partial(who, half, n):
        c = columns(n, 512)
        at = slice(half * 128, half * 128 + 128)
        return dot(dg[who, at, :], w[0, :, c], 1, 0) + dot(du[who, at, :], w[1, :, c], 1, 0)

    def dx_copy(half, h):
        at = slice(half * 16, half * 16 + 16)
        c = slice(h * 1024, h * 1024 + 1024)
        return remote(dxs.at[at, :, c], dxr.at[at, :, c], dx_s.at[half, h], dx_r.at[half, h], me, tpart)

    def send_partial(half):
        for h in range(2):
            def go(n, carry):
                dxs[half * 16 : half * 16 + 16, :, columns(n, 512)] = partial(1, half, n).astype(BF).reshape(16, 8, 512)
                return carry

            lax.fori_loop(2 * h, 2 * h + 2, go, 0)
            dx_copy(half, h).start()

    def own_partial(half):
        def go(n, carry):
            dxo[half * 128 : half * 128 + 128, columns(n, 512)] = partial(0, half, n)
            return carry

        lax.fori_loop(0, 4, go, 0)

    def give_back(half):
        at = slice(half * 16, half * 16 + 16)
        for h in range(2):
            dx_copy(half, h).wait()
            c = slice(h * 1024, h * 1024 + 1024)
            total = dxo[half * 128 : half * 128 + 128, c] + dxr[at, :, c].reshape(128, 1024).astype(F32)
            rets[at, :, c] = total.astype(BF).reshape(16, 8, 1024)

            def give(q, carry):
                e = (((z + 8 - offset(q // 4)) % 8) * 4 + q % 4) * 2 + h
                src = rets.at[q, :, c]

                @pl.when(e == me)
                def _():
                    local(src, retr.at[me], ret_r).start()

                @pl.when(e != me)
                def _():
                    remote(src, retr.at[me], ret_s, ret_r, e, s).start()

                return carry

            lax.fori_loop(half * 16, half * 16 + 16, give, 0)

    forward(0, 4)
    for k, src in enumerate((gw, uw, dw)):
        local(src, w.at[k, pl.ds(0, 192)], load_sem.at[3 + k]).wait()
        remote(src, w.at[k, pl.ds(192, 192)], wt_s.at[k], wt_r.at[k], me, wpart).wait()
    first(0, 0)
    forward(4, 6)
    wait_forward(0)
    first(1, 0)
    send_partial(0)
    own_partial(0)

    local(plan, planv, load_sem.at[2]).wait()
    spread = one(iota((64, 512), 0) == iota((64, 512), 1) // 8)
    held = dot(planv[...].astype(F32).astype(BF), spread, 1, 0)
    r = iota((384, 512), 0)
    mt[...] = one((r // 48 == iota((384, 512), 1) % 8) & ((r % 48).astype(F32) == held))

    forward(6, 8)
    first(0, 1)
    give_back(0)
    wait_forward(1)
    first(1, 1)

    u = iota((384, 384), 0)
    v = iota((384, 384), 1)
    turn = one((u // 192 == v // 192) & (u % 192 == (v % 64) * 3 + (v % 192) // 64))
    for who in range(2):
        hidt[:, who * 256 : (who + 1) * 256] = dot(turn, hid[who], 0, 1).astype(BF)

    def gsum(lo, n):
        c = columns(n, 512)
        out = dot(hidt[lo : lo + 192, 0:256], rows[1, 0, :, :, c].reshape(256, 512), 1, 0)
        return out + dot(hidt[lo : lo + 192, 256:512], rows[1, 1, :, :, c].reshape(256, 512), 1, 0)

    def gp_copy(j):
        at = slice(j * 64, j * 64 + 64)
        return remote(gsend.at[at], gpart.at[at], gp_s.at[j], gp_r.at[j], me, wpart)

    def other_grad(n, carry):
        gsend[:, columns(n, 512)] = gsum(192, n).astype(BF)
        return carry

    def own_grad(n, carry):
        gown[:, columns(n, 512)] = gsum(0, n)
        return carry

    lax.fori_loop(0, 4, other_grad, 0)
    for j in range(3):
        gp_copy(j).start()
    send_partial(1)
    lax.fori_loop(0, 4, own_grad, 0)
    own_partial(1)

    def exchange(src, dst, ss, rs, j):
        c = slice(j * 256, j * 256 + 256)

        def go(k, carry):
            zt = (z + offset(k // 8)) % 8
            e = (zt * 4 + (y + k // 2) % 4) * 2 + (core + k) % 2

            @pl.when(e == me)
            def _():
                local(src.at[e, :, c], dst.at[me, :, c], rs.at[j]).start()

            @pl.when(e != me)
            def _():
                remote(src.at[e, :, c], dst.at[me, :, c], ss, rs.at[j], e, s).start()

            return carry

        lax.fori_loop(0, 64, go, 0)

    def arrived(dst, rs, j):
        got = dst.at[:, :, j * 256 : j * 256 + 256]
        local(got, got, rs.at[j]).wait()

    a = iota((512, 512), 0)
    d = iota((512, 512), 1)
    weave = one((a // 8 == d % 64) & (a % 8 == d // 64))
    for j in range(3):
        gp_copy(j).wait()
        for b in range(8):
            c = slice(b * 256, (b + 1) * 256)
            at = slice(j * 64, j * 64 + 64)
            total = gown[at, c] + gpart[at, c].astype(F32)
            vst[j, b * 64 : (b + 1) * 64, :] = total.astype(BF)
        gs[:, :, j * 256 : j * 256 + 256] = dot(weave, vst[j], 1, 0).astype(BF).reshape(64, 8, 256)
        exchange(gs, grecv, ga_s, ga_r, j)

    give_back(1)

    for k, src in enumerate((mst, mom, sec)):
        local(src, states.at[k], load_sem.at[6 + k]).wait()
    results = (nms, nmo, nse)
    for j in range(3):
        cj = slice(j * 256, j * 256 + 256)
        arrived(grecv, ga_r, j)

        def update(b, carry):
            at = pl.ds(pl.multiple_of(b * 48, 48), 48)
            c = columns(b, 256)
            f = dot(mt[at, :], grecv[:, :, cj].reshape(512, 256), 1, 0)
            m0 = states[0, j, :, c]
            nm = 0.9 * states[1, j, :, c] + 0.1 * f
            ns = 0.95 * states[2, j, :, c] + 0.05 * f * f
            first_hat = nm / (1.0 - 0.9**10)
            second_hat = ns / (1.0 - 0.95**10)
            new = m0 - 0.01 * (first_hat / (jnp.sqrt(second_hat) + 1e-08) + 0.1 * m0)
            news[0, j, :, c] = new
            news[1, j, :, c] = nm
            news[2, j, :, c] = ns
            nmb[at, cj] = new.astype(BF)
            return carry

        lax.fori_loop(0, 8, update, 0)
        nds[:, :, cj] = dot(mt[...], nmb[:, cj], 0, 0).astype(BF).reshape(64, 8, 256)
        exchange(nds, ndr, nd_s, nd_r, j)
        for k in range(3):
            local(news.at[k, j], results[k].at[j], out_sem.at[3 * k + j]).start()

    local(retr, retr, ret_r).wait()
    place = one(iota((512, 256), 0).astype(F32) == pos[...])
    for n in range(2):
        c = slice(n * 512, (n + 1) * 512)
        tgv[:, :, c] = dot(place, retr[:, :, c].reshape(512, 512), 0, 0).astype(BF).reshape(2, 128, 512)
    mine = pl.ds(pl.multiple_of(core * 1024, 1024), 1024)
    tg_local = local(tgv.at[core], tg.at[:, mine], out_sem.at[9])
    tg_remote = remote(tgv.at[1 - core], tg.at[:, mine], tg_s, tg_r, other, s)
    tg_local.start()
    tg_remote.start()

    for j in range(3):
        arrived(ndr, nd_r, j)
        vst[j] = dot(weave, ndr[:, :, j * 256 : j * 256 + 256].reshape(512, 256), 0, 0).astype(BF)
    turn_back = one(iota((192, 192), 0) == (iota((192, 192), 1) % 64) * 3 + iota((192, 192), 1) // 64)
    for b in range(8):
        stack = [vst[j, b * 64 : (b + 1) * 64, :] for j in range(3)]
        ndo[:, b * 256 : (b + 1) * 256] = dot(turn_back, jnp.concatenate(stack, axis=0), 1, 0).astype(BF)
    last = local(ndo, nd, out_sem.at[10])
    last.start()

    for k in range(3):
        for j in range(3):
            local(news.at[k, j], results[k].at[j], out_sem.at[3 * k + j]).wait()
    tg_local.wait()
    tg_remote.wait()
    remote(sx.at[pl.ds(0, 63)], sx.at[pl.ds(0, 63)], disp_s, disp_s, other, s).wait_send()
    remote(span(0, 0, 32), span(0, 0, 32), fwd_s, fwd_s, me, tpart).wait_send()
    remote(retr.at[pl.ds(0, 63)], retr.at[pl.ds(0, 63)], ret_s, ret_s, other, s).wait_send()
    remote(gs.at[pl.ds(0, 63)], gs.at[pl.ds(0, 63)], ga_s, ga_s, other, s).wait_send()
    remote(nds.at[pl.ds(0, 63)], nds.at[pl.ds(0, 63)], nd_s, nd_s, other, s).wait_send()
    last.wait()


def body(tokens, out_grad, routing, plan, gate_weight, up_weight, down_weight, master, moment, second):
    any_ = pl.BlockSpec(memory_space=pl.ANY)
    vm = pltpu.VMEM
    dma = pltpu.SemaphoreType.DMA
    outs = pl.pallas_call(
        kernel,
        out_shape=(
            jax.ShapeDtypeStruct((128, 2048), BF),
            jax.ShapeDtypeStruct((3, 48, 2048), F32),
            jax.ShapeDtypeStruct((3, 48, 2048), F32),
            jax.ShapeDtypeStruct((3, 48, 2048), F32),
            jax.ShapeDtypeStruct((192, 2048), BF),
        ),
        in_specs=[any_] * 10,
        out_specs=[any_] * 5,
        scratch_shapes=[
            vm((2, 128, 2048), BF),
            vm((2, 1, 128), jnp.int32),
            vm((1, 256), F32),
            vm((64, 8, 2048), BF),
            vm((2, 2, 32, 8, 2048), BF),
            vm((3, 384, 2048), BF),
            vm((2, 256, 384), BF),
            vm((2, 256, 384), BF),
            vm((2, 256, 384), BF),
            vm((384, 512), BF),
            vm((32, 8, 2048), BF),
            vm((32, 8, 2048), BF),
            vm((256, 2048), F32),
            vm((32, 8, 2048), BF),
            vm((64, 8, 1024), BF),
            vm((2, 128, 1024), BF),
            vm((192, 2048), BF),
            vm((192, 2048), BF),
            vm((192, 2048), F32),
            vm((3, 512, 256), BF),
            vm((64, 8, 768), BF),
            vm((64, 8, 768), BF),
            vm((1, 64), jnp.int32),
            vm((384, 512), BF),
            vm((3, 3, 48, 2048), F32),
            vm((3, 3, 48, 2048), F32),
            vm((384, 768), BF),
            vm((64, 8, 768), BF),
            vm((64, 8, 768), BF),
            vm((192, 2048), BF),
            dma((9,)),
            dma((2,)), dma((2,)),
            dma, dma((32,)),
            dma, dma((2,)),
            dma((3,)), dma((3,)),
            dma((2, 2)), dma((2, 2)),
            dma, dma,
            dma, dma,
            dma((3,)), dma((3,)),
            dma, dma((3,)),
            dma, dma((3,)),
            dma((11,)),
        ],
        compiler_params=pltpu.CompilerParams(
            collective_id=0, has_side_effects=True, vmem_limit_bytes=60 * 1024 * 1024
        ),
    )(
        tokens,
        out_grad,
        routing.reshape(1, 128),
        plan.reshape(1, 64),
        jnp.transpose(gate_weight[0]),
        jnp.transpose(up_weight[0]),
        down_weight[0],
        jnp.transpose(master, (1, 0, 2)),
        jnp.transpose(moment, (1, 0, 2)),
        jnp.transpose(second, (1, 0, 2)),
    )
    token_grad, new_master, new_moment, new_second, new_down = outs
    back = lambda t: jnp.transpose(t, (1, 0, 2))
    return token_grad, back(new_master), back(new_moment), back(new_second), new_down[None]


def solution(mesh):
    placed = (
        P(("expert", "slot"), None),
        P(("expert", "slot"), None),
        P(("expert", "slot"), None),
        P(),
        P("expert", None, "slot"),
        P("expert", None, "slot"),
        P("expert", "slot", None),
        P(None, ("slot", "expert"), None),
        P(None, ("slot", "expert"), None),
        P(None, ("slot", "expert"), None),
    )
    return jax.shard_map(
        body,
        mesh=mesh,
        in_specs=placed,
        out_specs=(
            P(("expert", "slot"), None),
            P(None, ("slot", "expert"), None),
            P(None, ("slot", "expert"), None),
            P(None, ("slot", "expert"), None),
            P("expert", "slot", None),
        ),
        check_vma=False,
    )
```

```python
import functools

import jax
import jax.numpy as jnp
from jax import lax
from jax.experimental import pallas as pl
from jax.experimental.pallas import tpu as pltpu
from jax.sharding import PartitionSpec as P

MESH = pl.DeviceIdType.MESH
BF = jnp.bfloat16
F32 = jnp.float32


def dot(a, b, ca, cb):
    return lax.dot_general(a, b, (((ca,), (cb,)), ((), ())), preferred_element_type=F32)


def one(mask):
    return jnp.where(mask, 1.0, 0.0).astype(BF)


def iota(shape, dim):
    return lax.broadcasted_iota(jnp.int32, shape, dim)


def offset(i):
    h = i // 4
    j = (i + 3) % 4
    k = (i + 2) % 4
    near = 2 * ((j + 1) // 2) * (1 - 2 * (j % 2))
    far = (2 * (k // 2) + 1) * (2 * (k % 2) - 1)
    return 4 + (1 - h) * near + h * far


def kernel(
    tok, og, route, plan, gw, uw, dw, mst, mom, sec,
    tg, nms, nmo, nse, ndo,
    dense, routes, pos, sx, rows, w, hid, dg, du, hidt,
    dxs, dxr, dxo, rets, retr, tgv,
    gsend, gpart, gown, vst, gs, grecv, planv, mt, states, nmb, nds, ndr,
    load_sem, swap_s, swap_r, disp_s, disp_r, fwd_s, fwd_r, wt_s, wt_r,
    dx_s, dx_r, ret_s, ret_r, tg_s, tg_r, gp_s, gp_r, ga_s, ga_r, nd_s, nd_r, out_sem,
):
    me = lax.axis_index("expert")
    s = lax.axis_index("slot")
    core = me % 2
    chip = me // 2
    z = chip // 4
    y = chip % 4
    other = me + 1 - 2 * core
    low = s + 1 - 2 * (s % 2)
    high = (s + 1 + 2 * ((s + 1) % 2)) % 4
    tpart = low + core * (high - low)
    wpart = high + core * (low - high)

    def remote(src, dst, ss, rs, e, x):
        return pltpu.make_async_remote_copy(
            src_ref=src, dst_ref=dst, send_sem=ss, recv_sem=rs, device_id=(e, x), device_id_type=MESH
        )

    def local(src, dst, sem):
        return pltpu.make_async_copy(src, dst, sem)

    @pl.when(core == 0)
    def _():
        local(tok, dense.at[core], load_sem.at[0]).start()

    @pl.when(core == 1)
    def _():
        local(og, dense.at[core], load_sem.at[0]).start()

    local(route, routes.at[core], load_sem.at[1]).start()
    local(plan, planv, load_sem.at[2]).start()
    for k, src in enumerate((gw, uw, dw)):
        local(src, w.at[k, pl.ds(0, 192)], load_sem.at[3 + k]).start()
    for k, src in enumerate((mst, mom, sec)):
        local(src, states.at[k], load_sem.at[6 + k]).start()

    barrier = pltpu.get_barrier_semaphore()

    spot = {(dy, dc): ((y + dy) % 4) * 2 + (core + dc) % 2 for dy in range(4) for dc in range(2)}
    order = [(dy, dc) for dy in (2, 1, 3, 0) for dc in (1, 0)]

    def greet(i, carry):
        plane = ((z + 4 + ((i + 1) // 2) * (1 - 2 * (i % 2)) + 8) % 8) * 8
        for dy, dc in order:
            e = plane + spot[dy, dc]
            if (dy, dc) == (0, 0):
                @pl.when(e != me)
                def _():
                    pl.semaphore_signal(barrier, inc=1, device_id=(e, s), device_id_type=MESH)
            else:
                pl.semaphore_signal(barrier, inc=1, device_id=(e, s), device_id_type=MESH)
        return carry

    lax.fori_loop(0, 8, greet, 0)
    for x in (tpart, wpart):
        pl.semaphore_signal(barrier, inc=1, device_id=(me, x), device_id_type=MESH)
    pl.semaphore_wait(barrier, 65)

    @pl.when(core == 0)
    def _():
        remote(og, dense.at[core], swap_s.at[0], swap_r.at[0], other, s).start()

    @pl.when(core == 1)
    def _():
        remote(tok, dense.at[core], swap_s.at[0], swap_r.at[0], other, s).start()

    remote(route, routes.at[core], swap_s.at[1], swap_r.at[1], other, s).start()
    for k, src in enumerate((gw, uw, dw)):
        remote(src, w.at[k, pl.ds(192, 192)], wt_s.at[k], wt_r.at[k], me, wpart).start()

    local(route, routes.at[core], load_sem.at[1]).wait()
    remote(route, routes.at[core], swap_s.at[1], swap_r.at[1], other, s).wait()
    upper = one(iota((128, 128), 0) < iota((128, 128), 1))
    for c in range(2):
        hit = iota((64, 128), 0) == routes[c]
        before = dot(one(hit), upper, 1, 0)
        rank = jnp.sum(jnp.where(hit, before, 0.0), axis=0, keepdims=True)
        pos[:, c * 128 : (c + 1) * 128] = routes[c].astype(F32) * 8.0 + (c * 4.0) + rank

    local(tok, dense.at[core], load_sem.at[0]).wait()
    remote(tok, dense.at[core], swap_s.at[0], swap_r.at[0], other, s).wait()

    def dispatch(i, carry):
        zt = (z + offset(i)) % 8
        pick = one((iota((64, 256), 0) + zt * 64).astype(F32) == pos[...])
        block = dot(pick, dense[...].reshape(256, 2048), 1, 0).astype(BF)
        sx[pl.ds(zt * 8, 8)] = block.reshape(8, 8, 2048)
        q = i * 4 + y
        dst = rows.at[core, 0, q]
        for dy, dc in order:
            e = zt * 8 + spot[dy, dc]

            def send():
                remote(sx.at[e], dst, disp_s, disp_r.at[q], e, s).start()

            if (dy, dc) == (0, 0):
                @pl.when(i == 0)
                def _():
                    local(sx.at[e], dst, disp_r.at[q]).start()

                pl.when(i != 0)(send)
            else:
                send()
        return carry

    lax.fori_loop(0, 8, dispatch, 0)

    def span(who, q, n):
        return rows.at[:, who, pl.ds(q, n)]

    def forward(lo, hi):
        def go(i, carry):
            for dy in (2, 1, 3, 0):
                q = i * 4 + spot[4 - dy if dy else 0, 0] // 2
                local(span(0, q, 1), span(0, q, 1), disp_r.at[q]).wait()
                remote(span(0, q, 1), span(1, q, 1), fwd_s, fwd_r.at[i // 4], me, tpart).start()
            return carry

        lax.fori_loop(lo, hi, go, 0)

    def columns(n, size):
        return pl.ds(pl.multiple_of(n * size, size), size)

    def first(who, half):
        x = rows[0, who, half * 16 : half * 16 + 16].reshape(128, 2048)
        g = rows[1, who, half * 16 : half * 16 + 16].reshape(128, 2048)
        gate = dot(x, w[0], 1, 1)
        up = dot(x, w[1], 1, 1)
        dh = dot(g, w[2], 1, 1)
        sig = jax.nn.sigmoid(gate)
        silu = gate * sig
        at = slice(half * 128, half * 128 + 128)
        hid[who, at, :] = (silu * up).astype(BF)
        dg[who, at, :] = (dh * up * sig * (1.0 + gate * (1.0 - sig))).astype(BF)
        du[who, at, :] = (dh * silu).astype(BF)

    def wait_forward(half):
        remote(span(0, 0, 16), span(1, half * 16, 16), fwd_s, fwd_r.at[half], me, tpart).wait_recv()

    def partial(who, half, n):
        c = columns(n, 512)
        at = slice(half * 128, half * 128 + 128)
        return dot(dg[who, at, :], w[0, :, c], 1, 0) + dot(du[who, at, :], w[1, :, c], 1, 0)

    def dx_copy(half, h):
        at = slice(half * 16, half * 16 + 16)
        c = slice(h * 1024, h * 1024 + 1024)
        return remote(dxs.at[at, :, c], dxr.at[at, :, c], dx_s.at[half, h], dx_r.at[half, h], me, tpart)

    def send_partial(half):
        for h in range(2):
            def go(n, carry):
                dxs[half * 16 : half * 16 + 16, :, columns(n, 512)] = partial(1, half, n).astype(BF).reshape(16, 8, 512)
                return carry

            lax.fori_loop(2 * h, 2 * h + 2, go, 0)
            dx_copy(half, h).start()

    def own_partial(half):
        def go(n, carry):
            dxo[half * 128 : half * 128 + 128, columns(n, 512)] = partial(0, half, n)
            return carry

        lax.fori_loop(0, 4, go, 0)

    def give_back(half):
        at = slice(half * 16, half * 16 + 16)
        for h in range(2):
            dx_copy(half, h).wait()
            c = slice(h * 1024, h * 1024 + 1024)
            total = dxo[half * 128 : half * 128 + 128, c] + dxr[at, :, c].reshape(128, 1024).astype(F32)
            rets[at, :, c] = total.astype(BF).reshape(16, 8, 1024)

            def give(i, carry):
                plane = ((z + 8 - offset(i)) % 8) * 8
                for yy in range(4):
                    e = plane + yy * 2 + h
                    src = rets.at[i * 4 + yy, :, c]

                    def send():
                        remote(src, retr.at[me], ret_s, ret_r, e, s).start()

                    if half:
                        send()
                    else:
                        @pl.when(e == me)
                        def _():
                            local(src, retr.at[me], ret_r).start()

                        pl.when(e != me)(send)
                return carry

            lax.fori_loop(half * 4, half * 4 + 4, give, 0)

    forward(0, 4)
    for k, src in enumerate((gw, uw, dw)):
        local(src, w.at[k, pl.ds(0, 192)], load_sem.at[3 + k]).wait()
        remote(src, w.at[k, pl.ds(192, 192)], wt_s.at[k], wt_r.at[k], me, wpart).wait()
    first(0, 0)
    forward(4, 6)
    wait_forward(0)
    first(1, 0)
    send_partial(0)
    own_partial(0)

    local(plan, planv, load_sem.at[2]).wait()
    spread = one(iota((64, 512), 0) == iota((64, 512), 1) // 8)
    held = dot(planv[...].astype(F32).astype(BF), spread, 1, 0)
    r = iota((384, 512), 0)
    mt[...] = one((r // 48 == iota((384, 512), 1) % 8) & ((r % 48).astype(F32) == held))

    forward(6, 8)
    first(0, 1)
    give_back(0)
    wait_forward(1)
    first(1, 1)

    u = iota((384, 384), 0)
    v = iota((384, 384), 1)
    turn = one((u // 192 == v // 192) & (u % 192 == (v % 64) * 3 + (v % 192) // 64))
    for who in range(2):
        hidt[:, who * 256 : (who + 1) * 256] = dot(turn, hid[who], 0, 1).astype(BF)

    def gsum(lo, n):
        c = columns(n, 512)
        out = dot(hidt[lo : lo + 192, 0:256], rows[1, 0, :, :, c].reshape(256, 512), 1, 0)
        return out + dot(hidt[lo : lo + 192, 256:512], rows[1, 1, :, :, c].reshape(256, 512), 1, 0)

    def gp_copy(j):
        at = slice(j * 64, j * 64 + 64)
        return remote(gsend.at[at], gpart.at[at], gp_s.at[j], gp_r.at[j], me, wpart)

    def other_grad(n, carry):
        gsend[:, columns(n, 512)] = gsum(192, n).astype(BF)
        return carry

    def own_grad(n, carry):
        gown[:, columns(n, 512)] = gsum(0, n)
        return carry

    lax.fori_loop(0, 4, other_grad, 0)
    for j in range(3):
        gp_copy(j).start()
    send_partial(1)
    lax.fori_loop(0, 4, own_grad, 0)
    own_partial(1)

    def exchange(src, dst, ss, rs, j):
        c = slice(j * 256, j * 256 + 256)

        def go(i, carry):
            plane = ((z + offset(i)) % 8) * 8
            for dy, dc in order:
                e = plane + spot[dy, dc]

                def send():
                    remote(src.at[e, :, c], dst.at[me, :, c], ss, rs.at[j], e, s).start()

                if (dy, dc) == (0, 0):
                    @pl.when(i == 0)
                    def _():
                        local(src.at[e, :, c], dst.at[me, :, c], rs.at[j]).start()

                    pl.when(i != 0)(send)
                else:
                    send()
            return carry

        lax.fori_loop(0, 8, go, 0)

    def arrived(dst, rs, j):
        got = dst.at[:, :, j * 256 : j * 256 + 256]
        local(got, got, rs.at[j]).wait()

    a = iota((512, 512), 0)
    d = iota((512, 512), 1)
    weave = one((a // 8 == d % 64) & (a % 8 == d // 64))
    for j in range(3):
        gp_copy(j).wait()
        for b in range(8):
            c = slice(b * 256, (b + 1) * 256)
            at = slice(j * 64, j * 64 + 64)
            total = gown[at, c] + gpart[at, c].astype(F32)
            vst[j, b * 64 : (b + 1) * 64, :] = total.astype(BF)
        gs[:, :, j * 256 : j * 256 + 256] = dot(weave, vst[j], 1, 0).astype(BF).reshape(64, 8, 256)
        exchange(gs, grecv, ga_s, ga_r, j)

    give_back(1)

    for k, src in enumerate((mst, mom, sec)):
        local(src, states.at[k], load_sem.at[6 + k]).wait()
    for j in range(3):
        cj = slice(j * 256, j * 256 + 256)
        arrived(grecv, ga_r, j)

        def update(b, carry):
            at = pl.ds(pl.multiple_of(b * 48, 48), 48)
            c = columns(b, 256)
            f = dot(mt[at, :], grecv[:, :, cj].reshape(512, 256), 1, 0)
            m0 = states[0, j, :, c]
            nm = 0.9 * states[1, j, :, c] + 0.1 * f
            ns = 0.95 * states[2, j, :, c] + 0.05 * f * f
            first_hat = nm / (1.0 - 0.9**10)
            second_hat = ns / (1.0 - 0.95**10)
            new = m0 - 0.01 * (first_hat / (jnp.sqrt(second_hat) + 1e-08) + 0.1 * m0)
            nms[j, :, c] = new
            nmo[j, :, c] = nm
            nse[j, :, c] = ns
            nmb[at, cj] = new.astype(BF)
            return carry

        lax.fori_loop(0, 8, update, 0)
        nds[:, :, cj] = dot(mt[...], nmb[:, cj], 0, 0).astype(BF).reshape(64, 8, 256)
        exchange(nds, ndr, nd_s, nd_r, j)

    local(retr, retr, ret_r).wait()
    place = one(iota((512, 256), 0).astype(F32) == pos[...])
    for n in range(2):
        c = slice(n * 512, (n + 1) * 512)
        tgv[:, :, c] = dot(place, retr[:, :, c].reshape(512, 512), 0, 0).astype(BF).reshape(2, 128, 512)
    mine = pl.ds(pl.multiple_of(core * 1024, 1024), 1024)
    tg_local = local(tgv.at[core], tg.at[:, mine], out_sem)
    tg_remote = remote(tgv.at[1 - core], tg.at[:, mine], tg_s, tg_r, other, s)
    tg_local.start()
    tg_remote.start()

    for j in range(3):
        arrived(ndr, nd_r, j)
        vst[j] = dot(weave, ndr[:, :, j * 256 : j * 256 + 256].reshape(512, 256), 0, 0).astype(BF)
    turn_back = one(iota((192, 192), 0) == (iota((192, 192), 1) % 64) * 3 + iota((192, 192), 1) // 64)
    for b in range(8):
        stack = [vst[j, b * 64 : (b + 1) * 64, :] for j in range(3)]
        ndo[:, b * 256 : (b + 1) * 256] = dot(turn_back, jnp.concatenate(stack, axis=0), 1, 0).astype(BF)

    tg_local.wait()
    tg_remote.wait()
    remote(sx.at[pl.ds(0, 63)], sx.at[pl.ds(0, 63)], disp_s, disp_s, other, s).wait_send()
    remote(span(0, 0, 32), span(0, 0, 32), fwd_s, fwd_s, me, tpart).wait_send()
    remote(retr.at[pl.ds(0, 63)], retr.at[pl.ds(0, 63)], ret_s, ret_s, other, s).wait_send()
    remote(gs.at[pl.ds(0, 63)], gs.at[pl.ds(0, 63)], ga_s, ga_s, other, s).wait_send()
    remote(nds.at[pl.ds(0, 63)], nds.at[pl.ds(0, 63)], nd_s, nd_s, other, s).wait_send()


def store(*refs):
    sem = refs[-1]
    half = (len(refs) - 1) // 2
    copies = [pltpu.make_async_copy(refs[k], refs[half + k], sem.at[k]) for k in range(half)]
    for c in copies:
        c.start()
    for c in copies:
        c.wait()


def body(tokens, out_grad, routing, plan, gate_weight, up_weight, down_weight, master, moment, second):
    hbm = pl.BlockSpec(memory_space=pltpu.HBM)
    results = (
        ((128, 2048), BF),
        ((3, 48, 2048), F32),
        ((3, 48, 2048), F32),
        ((3, 48, 2048), F32),
        ((192, 2048), BF),
    )
    vm = pltpu.VMEM
    dma = pltpu.SemaphoreType.DMA
    outs = pl.pallas_call(
        kernel,
        out_shape=tuple(vm(shape, kind) for shape, kind in results),
        in_specs=[hbm] * 10,
        out_specs=[pl.BlockSpec(memory_space=pltpu.VMEM)] * 5,
        scratch_shapes=[
            vm((2, 128, 2048), BF),
            vm((2, 1, 128), jnp.int32),
            vm((1, 256), F32),
            vm((64, 8, 2048), BF),
            vm((2, 2, 32, 8, 2048), BF),
            vm((3, 384, 2048), BF),
            vm((2, 256, 384), BF),
            vm((2, 256, 384), BF),
            vm((2, 256, 384), BF),
            vm((384, 512), BF),
            vm((32, 8, 2048), BF),
            vm((32, 8, 2048), BF),
            vm((256, 2048), F32),
            vm((32, 8, 2048), BF),
            vm((64, 8, 1024), BF),
            vm((2, 128, 1024), BF),
            vm((192, 2048), BF),
            vm((192, 2048), BF),
            vm((192, 2048), F32),
            vm((3, 512, 256), BF),
            vm((64, 8, 768), BF),
            vm((64, 8, 768), BF),
            vm((1, 64), jnp.int32),
            vm((384, 512), BF),
            vm((3, 3, 48, 2048), F32),
            vm((384, 768), BF),
            vm((64, 8, 768), BF),
            vm((64, 8, 768), BF),
            dma((9,)),
            dma((2,)), dma((2,)),
            dma, dma((32,)),
            dma, dma((2,)),
            dma((3,)), dma((3,)),
            dma((2, 2)), dma((2, 2)),
            dma, dma,
            dma, dma,
            dma((3,)), dma((3,)),
            dma, dma((3,)),
            dma, dma((3,)),
            dma,
        ],
        compiler_params=pltpu.CompilerParams(
            collective_id=0, has_side_effects=True, vmem_limit_bytes=58 * 1024 * 1024
        ),
    )(
        tokens,
        out_grad,
        routing.reshape(1, 128),
        plan.reshape(1, 64),
        jnp.transpose(gate_weight[0]),
        jnp.transpose(up_weight[0]),
        down_weight[0],
        jnp.transpose(master, (1, 0, 2)),
        jnp.transpose(moment, (1, 0, 2)),
        jnp.transpose(second, (1, 0, 2)),
    )
    token_grad, new_master, new_moment, new_second, new_down = pl.pallas_call(
        store,
        out_shape=tuple(jax.ShapeDtypeStruct(shape, kind) for shape, kind in results),
        in_specs=[pl.BlockSpec(memory_space=pl.ANY)] * 5,
        out_specs=[hbm] * 5,
        scratch_shapes=[dma((5,))],
        compiler_params=pltpu.CompilerParams(vmem_limit_bytes=1024 * 1024),
    )(*outs)
    back = lambda t: jnp.transpose(t, (1, 0, 2))
    return token_grad, back(new_master), back(new_moment), back(new_second), new_down[None]


def solution(mesh):
    placed = (
        P(("expert", "slot"), None),
        P(("expert", "slot"), None),
        P(("expert", "slot"), None),
        P(),
        P("expert", None, "slot"),
        P("expert", None, "slot"),
        P("expert", "slot", None),
        P(None, ("slot", "expert"), None),
        P(None, ("slot", "expert"), None),
        P(None, ("slot", "expert"), None),
    )
    return jax.shard_map(
        body,
        mesh=mesh,
        in_specs=placed,
        out_specs=(
            P(("expert", "slot"), None),
            P(None, ("slot", "expert"), None),
            P(None, ("slot", "expert"), None),
            P(None, ("slot", "expert"), None),
            P("expert", "slot", None),
        ),
        check_vma=False,
    )
```

```python
import functools

import jax
import jax.numpy as jnp
from jax import lax
from jax.experimental import pallas as pl
from jax.experimental.pallas import tpu as pltpu
from jax.sharding import PartitionSpec as P

MESH = pl.DeviceIdType.MESH
BF = jnp.bfloat16
F32 = jnp.float32


def dot(a, b, ca, cb):
    return lax.dot_general(a, b, (((ca,), (cb,)), ((), ())), preferred_element_type=F32)


def one(mask):
    return jnp.where(mask, 1.0, 0.0).astype(BF)


def iota(shape, dim):
    return lax.broadcasted_iota(jnp.int32, shape, dim)


def offset(i):
    h = i // 4
    k = i % 4
    return (1 - h) * (3 + (k * (7 - 3 * k)) // 2) + h * (4 + (2 + k // 2) * (2 * (k % 2) - 1))


def kernel(
    tok, og, route, plan, gw, uw, dw, mst, mom, sec,
    tg, nms, nmo, nse, ndo,
    dense, routes, pos, sx, rows, w, hid, dg, du, hidt,
    dxs, dxr, dxo, rets, retr, tgv,
    gsend, gpart, gown, vst, gs, grecv, planv, mt, mtt, wv, wvt, turn, back, placet, gpre, states, nmb, nds, ndr,
    load_sem, swap_s, swap_r, disp_s, disp_r, fwd_s, fwd_r, wt_s, wt_r,
    dx_s, dx_r, ret_s, ret_r, tg_s, tg_r, gp_s, gp_r, ga_s, ga_r, nd_s, nd_r, out_sem,
):
    me = lax.axis_index("expert")
    s = lax.axis_index("slot")
    core = me % 2
    chip = me // 2
    z = chip // 4
    y = chip % 4
    other = me + 1 - 2 * core
    low = s + 1 - 2 * (s % 2)
    high = (s + 1 + 2 * ((s + 1) % 2)) % 4
    tpart = low + core * (high - low)
    wpart = high + core * (low - high)

    def remote(src, dst, ss, rs, e, x):
        return pltpu.make_async_remote_copy(
            src_ref=src, dst_ref=dst, send_sem=ss, recv_sem=rs, device_id=(e, x), device_id_type=MESH
        )

    def local(src, dst, sem):
        return pltpu.make_async_copy(src, dst, sem)

    @pl.when(core == 0)
    def _():
        local(tok, dense.at[core], load_sem.at[0]).start()

    @pl.when(core == 1)
    def _():
        local(og, dense.at[core], load_sem.at[0]).start()

    local(route, routes.at[core], load_sem.at[1]).start()
    local(plan, planv, load_sem.at[2]).start()
    for k, src in enumerate((gw, uw, dw)):
        local(src, w.at[k, pl.ds(0, 192)], load_sem.at[3 + k]).start()
    for k, src in enumerate((mst, mom, sec)):
        local(src, states.at[k], load_sem.at[6 + k]).start()

    barrier = pltpu.get_barrier_semaphore()

    spot = {(dy, dc): ((y + dy) % 4) * 2 + (core + dc) % 2 for dy in range(4) for dc in range(2)}
    order = [(dy, dc) for dy in (2, 1, 3, 0) for dc in (1, 0)]

    def greet(i, carry):
        plane = ((z + 4 + ((i + 1) // 2) * (1 - 2 * (i % 2)) + 8) % 8) * 8
        for dy, dc in order:
            e = plane + spot[dy, dc]
            if (dy, dc) == (0, 0):
                @pl.when(e != me)
                def _():
                    pl.semaphore_signal(barrier, inc=1, device_id=(e, s), device_id_type=MESH)
            else:
                pl.semaphore_signal(barrier, inc=1, device_id=(e, s), device_id_type=MESH)
        return carry

    lax.fori_loop(0, 8, greet, 0)
    for x in (tpart, wpart):
        pl.semaphore_signal(barrier, inc=1, device_id=(me, x), device_id_type=MESH)
    pl.semaphore_wait(barrier, 65)

    @pl.when(core == 0)
    def _():
        remote(og, dense.at[core], swap_s.at[0], swap_r.at[0], other, s).start()

    @pl.when(core == 1)
    def _():
        remote(tok, dense.at[core], swap_s.at[0], swap_r.at[0], other, s).start()

    remote(route, routes.at[core], swap_s.at[1], swap_r.at[1], other, s).start()
    for k, src in enumerate((gw, uw, dw)):
        remote(src, w.at[k, pl.ds(192, 192)], wt_s.at[k], wt_r.at[k], me, wpart).start()

    local(route, routes.at[core], load_sem.at[1]).wait()
    remote(route, routes.at[core], swap_s.at[1], swap_r.at[1], other, s).wait()
    upper = one(iota((128, 128), 0) < iota((128, 128), 1))
    for c in range(2):
        hit = iota((64, 128), 0) == routes[c]
        before = dot(one(hit), upper, 1, 0)
        rank = jnp.sum(jnp.where(hit, before, 0.0), axis=0, keepdims=True)
        pos[:, c * 128 : (c + 1) * 128] = routes[c].astype(F32) * 8.0 + (c * 4.0) + rank

    local(tok, dense.at[core], load_sem.at[0]).wait()
    remote(tok, dense.at[core], swap_s.at[0], swap_r.at[0], other, s).wait()

    def selections():
        spread = one(iota((64, 512), 0) == iota((64, 512), 1) // 8)
        held = dot(planv[...].astype(F32).astype(BF), spread, 1, 0)
        r = iota((384, 512), 0)
        m = jnp.where((r // 48 == iota((384, 512), 1) % 8) & ((r % 48).astype(F32) == held), 1.0, 0.0)
        mt[...] = m.astype(BF)
        mtt[...] = jnp.transpose(m).astype(BF)
        a = iota((512, 512), 0)
        d = iota((512, 512), 1)
        wv[...] = one((a // 8 == d % 64) & (a % 8 == d // 64))
        wvt[...] = one((d // 8 == a % 64) & (d % 8 == a // 64))
        u = iota((384, 384), 1)
        v = iota((384, 384), 0)
        turn[...] = one((u // 192 == v // 192) & (u % 192 == (v % 64) * 3 + (v % 192) // 64))
        for j in range(3):
            back[j] = one(iota((192, 64), 0) == iota((192, 64), 1) * 3 + j)
        place = jnp.where(iota((512, 256), 0).astype(F32) == pos[...], 1.0, 0.0)
        placet[...] = jnp.transpose(place).astype(BF)

    def dispatch(i, carry):
        zt = (z + offset(i)) % 8
        pick = one((iota((64, 256), 0) + zt * 64).astype(F32) == pos[...])
        block = dot(pick, dense[...].reshape(256, 2048), 1, 0).astype(BF)
        sx[pl.ds(zt * 8, 8)] = block.reshape(8, 8, 2048)
        q = i * 4 + y
        dst = rows.at[core, 0, q]
        for dy, dc in order:
            e = zt * 8 + spot[dy, dc]

            def send():
                remote(sx.at[e], dst, disp_s, disp_r.at[q], e, s).start()

            if (dy, dc) == (0, 0):
                @pl.when(i == 3)
                def _():
                    local(sx.at[e], dst, disp_r.at[q]).start()

                pl.when(i != 3)(send)
            else:
                send()
        return carry

    lax.fori_loop(0, 8, dispatch, 0)

    def span(who, q, n):
        return rows.at[:, who, pl.ds(q, n)]

    batches = ((0, 8), (8, 16), (16, 32))
    parts = ((0, 8), (8, 16), (16, 32))

    def forward(steps, dys=(2, 1, 3, 0)):
        for dy in dys:
            for i in steps:
                q = i * 4 + spot[(4 - dy) % 4, 0] // 2
                local(span(0, q, 1), span(0, q, 1), disp_r.at[q]).wait()
                remote(span(0, q, 1), span(1, q, 1), fwd_s, fwd_r.at[min(i // 2, 2)], me, tpart).start()

    def columns(n, size):
        return pl.ds(pl.multiple_of(n * size, size), size)

    def first(who, k):
        lo, hi = batches[k]
        count = (hi - lo) * 8
        x = rows[0, who, lo:hi].reshape(count, 2048)
        g = rows[1, who, lo:hi].reshape(count, 2048)
        gate = dot(x, w[0], 1, 1)
        up = dot(x, w[1], 1, 1)
        dh = dot(g, w[2], 1, 1)
        sig = jax.nn.sigmoid(gate)
        silu = gate * sig
        at = slice(lo * 8, hi * 8)
        hid[who, at, :] = (silu * up).astype(BF)
        dg[who, at, :] = (dh * up * sig * (1.0 + gate * (1.0 - sig))).astype(BF)
        du[who, at, :] = (dh * silu).astype(BF)

    def wait_forward(k):
        lo, hi = batches[k]
        remote(span(0, lo, hi - lo), span(1, lo, hi - lo), fwd_s, fwd_r.at[k], me, tpart).wait_recv()

    def partial(who, k, n):
        lo, hi = parts[k]
        c = columns(n, 512)
        at = slice(lo * 8, hi * 8)
        return dot(dg[who, at, :], w[0, :, c], 1, 0) + dot(du[who, at, :], w[1, :, c], 1, 0)

    def dx_copy(k, h):
        lo, hi = parts[k]
        c = slice(h * 1024, h * 1024 + 1024)
        return remote(dxs.at[lo:hi, :, c], dxr.at[lo:hi, :, c], dx_s.at[k, h], dx_r.at[k, h], me, tpart)

    def send_partial(k, halves=(0, 1)):
        lo, hi = parts[k]
        for h in halves:
            def go(n, carry):
                dxs[lo:hi, :, columns(n, 512)] = partial(1, k, n).astype(BF).reshape(hi - lo, 8, 512)
                return carry

            lax.fori_loop(2 * h, 2 * h + 2, go, 0)
            dx_copy(k, h).start()

    def own_partial(k):
        lo, hi = parts[k]

        def go(n, carry):
            dxo[lo * 8 : hi * 8, columns(n, 512)] = partial(0, k, n)
            return carry

        lax.fori_loop(0, 4, go, 0)

    def give_back(k):
        lo, hi = parts[k]
        for h in range(2):
            dx_copy(k, h).wait()
            c = slice(h * 1024, h * 1024 + 1024)
            total = dxo[lo * 8 : hi * 8, c] + dxr[lo:hi, :, c].reshape((hi - lo) * 8, 1024).astype(F32)
            rets[lo:hi, :, c] = total.astype(BF).reshape(hi - lo, 8, 1024)

            def give(i, carry):
                plane = ((z + 8 - offset(i)) % 8) * 8
                for yy in range(4):
                    e = plane + yy * 2 + h
                    src = rets.at[i * 4 + yy, :, c]

                    def send():
                        remote(src, retr.at[me], ret_s, ret_r, e, s).start()

                    if k != 1:
                        send()
                    else:
                        @pl.when(e == me)
                        def _():
                            local(src, retr.at[me], ret_r).start()

                        pl.when(e != me)(send)
                return carry

            lax.fori_loop(lo // 4, hi // 4, give, 0)

    def transpose(who, lo, hi):
        hidt[:, who * 256 + lo : who * 256 + hi] = dot(turn[...], hid[who, lo:hi, :], 1, 1).astype(BF)

    def gsum(lo, who, first_row, last_row, n):
        c = columns(n, 512)
        g = rows[1, who, first_row // 8 : last_row // 8, :, c].reshape(last_row - first_row, 512)
        return dot(hidt[lo : lo + 192, who * 256 + first_row : who * 256 + last_row], g, 1, 0)

    def early_grad(n, carry):
        gpre[:, columns(n, 512)] = gsum(192, 0, 0, 256, n) + gsum(192, 1, 0, 128, n)
        return carry

    def other_grad(n, carry):
        c = columns(n, 512)
        gsend[:, c] = (gpre[:, c] + gsum(192, 1, 128, 256, n)).astype(BF)
        return carry

    def own_grad(n, carry):
        gown[:, columns(n, 512)] = gsum(0, 0, 0, 256, n) + gsum(0, 1, 0, 256, n)
        return carry

    forward((3,))
    local(plan, planv, load_sem.at[2]).wait()
    selections()
    forward((0, 1))
    forward((2,))
    for k, src in enumerate((gw, uw, dw)):
        local(src, w.at[k, pl.ds(0, 192)], load_sem.at[3 + k]).wait()
        remote(src, w.at[k, pl.ds(192, 192)], wt_s.at[k], wt_r.at[k], me, wpart).wait()
    forward((4, 5), (2,))
    first(0, 0)
    wait_forward(0)
    first(1, 0)
    send_partial(0)
    forward((4, 5), (1, 3))
    own_partial(0)
    forward((4, 5), (0,))
    first(0, 1)
    wait_forward(1)
    first(1, 1)
    send_partial(1)
    forward((6, 7), (2, 1))
    give_back(0)
    forward((6, 7), (3, 0))
    own_partial(1)
    transpose(1, 0, 128)
    first(0, 2)
    transpose(0, 0, 256)
    lax.fori_loop(0, 4, early_grad, 0)
    give_back(1)
    wait_forward(2)
    first(1, 2)
    transpose(1, 128, 256)

    def gp_copy(j):
        at = slice(j * 64, j * 64 + 64)
        return remote(gsend.at[at], gpart.at[at], gp_s.at[j], gp_r.at[j], me, wpart)

    lax.fori_loop(0, 4, other_grad, 0)
    for j in range(3):
        gp_copy(j).start()
    lax.fori_loop(0, 4, own_grad, 0)

    def exchange(src, dst, ss, rs, j):
        c = slice(j * 256, j * 256 + 256)

        def go(i, carry):
            plane = ((z + offset(i)) % 8) * 8
            for dy, dc in order:
                e = plane + spot[dy, dc]

                def send():
                    remote(src.at[e, :, c], dst.at[me, :, c], ss, rs.at[j], e, s).start()

                if (dy, dc) == (0, 0):
                    @pl.when(i == 3)
                    def _():
                        local(src.at[e, :, c], dst.at[me, :, c], rs.at[j]).start()

                    pl.when(i != 3)(send)
                else:
                    send()
            return carry

        lax.fori_loop(0, 8, go, 0)

    def arrived(dst, rs, j):
        got = dst.at[:, :, j * 256 : j * 256 + 256]
        local(got, got, rs.at[j]).wait()

    for j in range(3):
        gp_copy(j).wait()
        for b in range(8):
            c = slice(b * 256, (b + 1) * 256)
            at = slice(j * 64, j * 64 + 64)
            total = gown[at, c] + gpart[at, c].astype(F32)
            vst[j, b * 64 : (b + 1) * 64, :] = total.astype(BF)
        gs[:, :, j * 256 : j * 256 + 256] = dot(wv[...], vst[j], 1, 0).astype(BF).reshape(64, 8, 256)
        exchange(gs, grecv, ga_s, ga_r, j)
        if j < 2:
            send_partial(2, (j,))
        else:
            own_partial(2)

    for k, src in enumerate((mst, mom, sec)):
        local(src, states.at[k], load_sem.at[6 + k]).wait()
    for j in range(3):
        cj = slice(j * 256, j * 256 + 256)
        if j == 1:
            give_back(2)
        arrived(grecv, ga_r, j)

        def update(b, carry):
            at = pl.ds(pl.multiple_of(b * 48, 48), 48)
            c = columns(b, 256)
            f = dot(mt[at, :], grecv[:, :, cj].reshape(512, 256), 1, 0)
            m0 = states[0, j, :, c]
            nm = 0.9 * states[1, j, :, c] + 0.1 * f
            ns = 0.95 * states[2, j, :, c] + 0.05 * f * f
            first_hat = nm / (1.0 - 0.9**10)
            second_hat = ns / (1.0 - 0.95**10)
            new = m0 - 0.01 * (first_hat / (jnp.sqrt(second_hat) + 1e-08) + 0.1 * m0)
            nms[j, :, c] = new
            nmo[j, :, c] = nm
            nse[j, :, c] = ns
            nmb[at, cj] = new.astype(BF)
            return carry

        lax.fori_loop(0, 8, update, 0)
        nds[:, :, cj] = dot(mtt[...], nmb[:, cj], 1, 0).astype(BF).reshape(64, 8, 256)
        exchange(nds, ndr, nd_s, nd_r, j)

    local(retr, retr, ret_r).wait()
    for n in range(2):
        c = slice(n * 512, (n + 1) * 512)
        tgv[:, :, c] = dot(placet[...], retr[:, :, c].reshape(512, 512), 1, 0).astype(BF).reshape(2, 128, 512)
    mine = pl.ds(pl.multiple_of(core * 1024, 1024), 1024)
    tg_local = local(tgv.at[core], tg.at[:, mine], out_sem)
    tg_remote = remote(tgv.at[1 - core], tg.at[:, mine], tg_s, tg_r, other, s)
    tg_local.start()
    tg_remote.start()

    for j in range(3):
        arrived(ndr, nd_r, j)
        vst[j] = dot(wvt[...], ndr[:, :, j * 256 : j * 256 + 256].reshape(512, 256), 1, 0).astype(BF)
        for b in range(8):
            c = slice(b * 256, (b + 1) * 256)
            put = dot(back[j], vst[j, b * 64 : (b + 1) * 64, :], 1, 0)
            if j == 0:
                gpre[:, c] = put
            elif j == 1:
                gpre[:, c] += put
            else:
                ndo[:, c] = (gpre[:, c] + put).astype(BF)

    tg_local.wait()
    tg_remote.wait()
    remote(sx.at[pl.ds(0, 63)], sx.at[pl.ds(0, 63)], disp_s, disp_s, other, s).wait_send()
    remote(span(0, 0, 32), span(0, 0, 32), fwd_s, fwd_s, me, tpart).wait_send()
    remote(retr.at[pl.ds(0, 63)], retr.at[pl.ds(0, 63)], ret_s, ret_s, other, s).wait_send()
    remote(gs.at[pl.ds(0, 63)], gs.at[pl.ds(0, 63)], ga_s, ga_s, other, s).wait_send()
    remote(nds.at[pl.ds(0, 63)], nds.at[pl.ds(0, 63)], nd_s, nd_s, other, s).wait_send()


def store(*refs):
    sem = refs[-1]
    half = (len(refs) - 1) // 2
    copies = [pltpu.make_async_copy(refs[k], refs[half + k], sem.at[k]) for k in range(half)]
    for c in copies:
        c.start()
    for c in copies:
        c.wait()


def body(tokens, out_grad, routing, plan, gate_weight, up_weight, down_weight, master, moment, second):
    hbm = pl.BlockSpec(memory_space=pltpu.HBM)
    results = (
        ((128, 2048), BF),
        ((3, 48, 2048), F32),
        ((3, 48, 2048), F32),
        ((3, 48, 2048), F32),
        ((192, 2048), BF),
    )
    vm = pltpu.VMEM
    dma = pltpu.SemaphoreType.DMA
    outs = pl.pallas_call(
        kernel,
        out_shape=tuple(vm(shape, kind) for shape, kind in results),
        in_specs=[hbm] * 10,
        out_specs=[pl.BlockSpec(memory_space=pltpu.VMEM)] * 5,
        scratch_shapes=[
            vm((2, 128, 2048), BF),
            vm((2, 1, 128), jnp.int32),
            vm((1, 256), F32),
            vm((64, 8, 2048), BF),
            vm((2, 2, 32, 8, 2048), BF),
            vm((3, 384, 2048), BF),
            vm((2, 256, 384), BF),
            vm((2, 256, 384), BF),
            vm((2, 256, 384), BF),
            vm((384, 512), BF),
            vm((32, 8, 2048), BF),
            vm((32, 8, 2048), BF),
            vm((256, 2048), F32),
            vm((32, 8, 2048), BF),
            vm((64, 8, 1024), BF),
            vm((2, 128, 1024), BF),
            vm((192, 2048), BF),
            vm((192, 2048), BF),
            vm((192, 2048), F32),
            vm((3, 512, 256), BF),
            vm((64, 8, 768), BF),
            vm((64, 8, 768), BF),
            vm((1, 64), jnp.int32),
            vm((384, 512), BF),
            vm((512, 384), BF),
            vm((512, 512), BF),
            vm((512, 512), BF),
            vm((384, 384), BF),
            vm((3, 192, 64), BF),
            vm((256, 512), BF),
            vm((192, 2048), F32),
            vm((3, 3, 48, 2048), F32),
            vm((384, 768), BF),
            vm((64, 8, 768), BF),
            vm((64, 8, 768), BF),
            dma((9,)),
            dma((2,)), dma((2,)),
            dma, dma((32,)),
            dma, dma((3,)),
            dma((3,)), dma((3,)),
            dma((3, 2)), dma((3, 2)),
            dma, dma,
            dma, dma,
            dma((3,)), dma((3,)),
            dma, dma((3,)),
            dma, dma((3,)),
            dma,
        ],
        compiler_params=pltpu.CompilerParams(
            collective_id=0, has_side_effects=True, vmem_limit_bytes=58 * 1024 * 1024
        ),
    )(
        tokens,
        out_grad,
        routing.reshape(1, 128),
        plan.reshape(1, 64),
        jnp.transpose(gate_weight[0]),
        jnp.transpose(up_weight[0]),
        down_weight[0],
        jnp.transpose(master, (1, 0, 2)),
        jnp.transpose(moment, (1, 0, 2)),
        jnp.transpose(second, (1, 0, 2)),
    )
    token_grad, new_master, new_moment, new_second, new_down = pl.pallas_call(
        store,
        out_shape=tuple(jax.ShapeDtypeStruct(shape, kind) for shape, kind in results),
        in_specs=[pl.BlockSpec(memory_space=pl.ANY)] * 5,
        out_specs=[hbm] * 5,
        scratch_shapes=[dma((5,))],
        compiler_params=pltpu.CompilerParams(vmem_limit_bytes=1024 * 1024),
    )(*outs)
    back = lambda t: jnp.transpose(t, (1, 0, 2))
    return token_grad, back(new_master), back(new_moment), back(new_second), new_down[None]


def solution(mesh):
    placed = (
        P(("expert", "slot"), None),
        P(("expert", "slot"), None),
        P(("expert", "slot"), None),
        P(),
        P("expert", None, "slot"),
        P("expert", None, "slot"),
        P("expert", "slot", None),
        P(None, ("slot", "expert"), None),
        P(None, ("slot", "expert"), None),
        P(None, ("slot", "expert"), None),
    )
    return jax.shard_map(
        body,
        mesh=mesh,
        in_specs=placed,
        out_specs=(
            P(("expert", "slot"), None),
            P(None, ("slot", "expert"), None),
            P(None, ("slot", "expert"), None),
            P(None, ("slot", "expert"), None),
            P("expert", "slot", None),
        ),
        check_vma=False,
    )
```

```python
import functools

import jax
import jax.numpy as jnp
from jax import lax
from jax.experimental import pallas as pl
from jax.experimental.pallas import tpu as pltpu
from jax.sharding import PartitionSpec as P

MESH = pl.DeviceIdType.MESH
BF = jnp.bfloat16
F32 = jnp.float32


def dot(a, b, ca, cb):
    return lax.dot_general(a, b, (((ca,), (cb,)), ((), ())), preferred_element_type=F32)


def one(mask):
    return jnp.where(mask, 1.0, 0.0).astype(BF)


def iota(shape, dim):
    return lax.broadcasted_iota(jnp.int32, shape, dim)


def offset(i):
    h = i // 4
    k = i % 4
    return (1 - h) * (3 + (k * (7 - 3 * k)) // 2) + h * (4 + (2 + k // 2) * (2 * (k % 2) - 1))


def kernel(
    tok, og, route, plan, gw, uw, dw, mst, mom, sec,
    tg, nms, nmo, nse, ndo,
    dense, routes, pos, sx, rows, w, hid, dg, du, hidt,
    dxs, dxr, dxo, rets, retr, tgv,
    gsend, gpart, gown, vst, gs, grecv, planv, mt, mtt, wv, wvt, turn, back, placet, gpre, kept, states, nmb, nds, ndr,
    load_sem, swap_s, swap_r, disp_s, disp_r, fwd_s, fwd_r, wt_s, wt_r,
    dx_s, dx_r, ret_s, ret_r, tg_s, tg_r, gp_s, gp_r, ga_s, ga_r, nd_s, nd_r, out_sem,
):
    me = lax.axis_index("expert")
    s = lax.axis_index("slot")
    core = me % 2
    chip = me // 2
    z = chip // 4
    y = chip % 4
    other = me + 1 - 2 * core
    low = s + 1 - 2 * (s % 2)
    high = (s + 1 + 2 * ((s + 1) % 2)) % 4
    tpart = low + core * (high - low)
    wpart = high + core * (low - high)

    def remote(src, dst, ss, rs, e, x):
        return pltpu.make_async_remote_copy(
            src_ref=src, dst_ref=dst, send_sem=ss, recv_sem=rs, device_id=(e, x), device_id_type=MESH
        )

    def local(src, dst, sem):
        return pltpu.make_async_copy(src, dst, sem)

    barrier = pltpu.get_barrier_semaphore()

    spot = {(dy, dc): ((y + dy) % 4) * 2 + (core + dc) % 2 for dy in range(4) for dc in range(2)}
    order = [(dy, dc) for dy in (2, 1, 3, 0) for dc in (1, 0)]

    def greet(i, carry):
        plane = ((z + 4 + ((i + 1) // 2) * (1 - 2 * (i % 2)) + 8) % 8) * 8
        for dy, dc in order:
            e = plane + spot[dy, dc]
            if (dy, dc) == (0, 0):
                @pl.when(e != me)
                def _():
                    pl.semaphore_signal(barrier, inc=1, device_id=(e, s), device_id_type=MESH)
            else:
                pl.semaphore_signal(barrier, inc=1, device_id=(e, s), device_id_type=MESH)
        return carry

    lax.fori_loop(0, 8, greet, 0)
    for x in (tpart, wpart):
        pl.semaphore_signal(barrier, inc=1, device_id=(me, x), device_id_type=MESH)

    @pl.when(core == 0)
    def _():
        local(tok, dense.at[core], load_sem.at[0]).start()

    @pl.when(core == 1)
    def _():
        local(og, dense.at[core], load_sem.at[0]).start()

    local(route, routes.at[core], load_sem.at[1]).start()
    local(plan, planv, load_sem.at[2]).start()
    for k, src in enumerate((gw, uw, dw)):
        local(src, w.at[k, pl.ds(0, 192)], load_sem.at[3 + k]).start()
    for k, src in enumerate((mst, mom, sec)):
        local(src, states.at[k], load_sem.at[6 + k]).start()

    pl.semaphore_wait(barrier, 65)

    @pl.when(core == 0)
    def _():
        remote(og, dense.at[core], swap_s.at[0], swap_r.at[0], other, s).start()

    @pl.when(core == 1)
    def _():
        remote(tok, dense.at[core], swap_s.at[0], swap_r.at[0], other, s).start()

    remote(route, routes.at[core], swap_s.at[1], swap_r.at[1], other, s).start()
    for k, src in enumerate((gw, uw, dw)):
        remote(src, w.at[k, pl.ds(192, 192)], wt_s.at[k], wt_r.at[k], me, wpart).start()

    local(route, routes.at[core], load_sem.at[1]).wait()
    remote(route, routes.at[core], swap_s.at[1], swap_r.at[1], other, s).wait()
    upper = one(iota((128, 128), 0) < iota((128, 128), 1))
    for c in range(2):
        hit = iota((64, 128), 0) == routes[c]
        before = dot(one(hit), upper, 1, 0)
        rank = jnp.sum(jnp.where(hit, before, 0.0), axis=0, keepdims=True)
        pos[:, c * 128 : (c + 1) * 128] = routes[c].astype(F32) * 8.0 + (c * 4.0) + rank

    local(tok, dense.at[core], load_sem.at[0]).wait()
    remote(tok, dense.at[core], swap_s.at[0], swap_r.at[0], other, s).wait()

    def selections():
        spread = one(iota((64, 512), 0) == iota((64, 512), 1) // 8)
        held = dot(planv[...].astype(F32).astype(BF), spread, 1, 0)
        r = iota((384, 512), 0)
        m = jnp.where((r // 48 == iota((384, 512), 1) % 8) & ((r % 48).astype(F32) == held), 1.0, 0.0)
        mt[...] = m.astype(BF)
        mtt[...] = jnp.transpose(m).astype(BF)
        a = iota((512, 512), 0)
        d = iota((512, 512), 1)
        wv[...] = one((a // 8 == d % 64) & (a % 8 == d // 64))
        wvt[...] = one((d // 8 == a % 64) & (d % 8 == a // 64))
        u = iota((384, 384), 1)
        v = iota((384, 384), 0)
        turn[...] = one((u // 192 == v // 192) & (u % 192 == (v % 64) * 3 + (v % 192) // 64))
        for j in range(3):
            back[j] = one(iota((192, 64), 0) == iota((192, 64), 1) * 3 + j)
        place = jnp.where(iota((512, 256), 0).astype(F32) == pos[...], 1.0, 0.0)
        placet[...] = jnp.transpose(place).astype(BF)

    def dispatch(i, carry):
        zt = (z + offset(i)) % 8
        pick = one((iota((64, 256), 0) + zt * 64).astype(F32) == pos[...])
        block = dot(pick, dense[...].reshape(256, 2048), 1, 0).astype(BF)
        sx[pl.ds(zt * 8, 8)] = block.reshape(8, 8, 2048)
        q = i * 4 + y
        dst = rows.at[core, 0, q]
        for dy, dc in order:
            e = zt * 8 + spot[dy, dc]

            def send():
                remote(sx.at[e], dst, disp_s, disp_r.at[q], e, s).start()

            if (dy, dc) == (0, 0):
                @pl.when(i == 3)
                def _():
                    local(sx.at[e], dst, disp_r.at[q]).start()

                pl.when(i != 3)(send)
            else:
                send()
        return carry

    lax.fori_loop(0, 8, dispatch, 0)

    def span(who, q, n):
        return rows.at[:, who, pl.ds(q, n)]

    batches = ((0, 16), (16, 32))
    parts = ((0, 12), (12, 32))

    def forward(steps, dys=(2, 1, 3, 0)):
        for dy in dys:
            for i in steps:
                q = i * 4 + spot[(4 - dy) % 4, 0] // 2
                local(span(0, q, 1), span(0, q, 1), disp_r.at[q]).wait()
                remote(span(0, q, 1), span(1, q, 1), fwd_s, fwd_r.at[i // 4], me, tpart).start()

    def columns(n, size):
        return pl.ds(pl.multiple_of(n * size, size), size)

    def project(who, k):
        lo, hi = batches[k]
        x = rows[0, who, lo:hi].reshape((hi - lo) * 8, 2048)
        gate = dot(x, w[0], 1, 1)
        up = dot(x, w[1], 1, 1)
        silu = gate * jax.nn.sigmoid(gate)
        hid[who, lo * 8 : hi * 8, :] = (silu * up).astype(BF)
        return gate, up

    def descend(who, k, gate, up):
        lo, hi = batches[k]
        g = rows[1, who, lo:hi].reshape((hi - lo) * 8, 2048)
        dh = dot(g, w[2], 1, 1)
        sig = jax.nn.sigmoid(gate)
        at = slice(lo * 8, hi * 8)
        dg[who, at, :] = (dh * up * sig * (1.0 + gate * (1.0 - sig))).astype(BF)
        du[who, at, :] = (dh * (gate * sig)).astype(BF)

    def first(who, k):
        descend(who, k, *project(who, k))

    def wait_forward(k):
        lo, hi = batches[k]
        remote(span(0, lo, hi - lo), span(1, lo, hi - lo), fwd_s, fwd_r.at[k], me, tpart).wait_recv()

    def partial(who, k, n):
        lo, hi = parts[k]
        c = columns(n, 512)
        at = slice(lo * 8, hi * 8)
        return dot(dg[who, at, :], w[0, :, c], 1, 0) + dot(du[who, at, :], w[1, :, c], 1, 0)

    def dx_copy(k, h):
        lo, hi = parts[k]
        c = slice(h * 1024, h * 1024 + 1024)
        return remote(dxs.at[lo:hi, :, c], dxr.at[lo:hi, :, c], dx_s.at[k, h], dx_r.at[k, h], me, tpart)

    def send_partial(k, halves=(0, 1)):
        lo, hi = parts[k]
        for h in halves:
            def go(n, carry):
                dxs[lo:hi, :, columns(n, 512)] = partial(1, k, n).astype(BF).reshape(hi - lo, 8, 512)
                return carry

            lax.fori_loop(2 * h, 2 * h + 2, go, 0)
            dx_copy(k, h).start()

    def own_partial(k):
        lo, hi = parts[k]

        def go(n, carry):
            dxo[lo * 8 : hi * 8, columns(n, 512)] = partial(0, k, n)
            return carry

        lax.fori_loop(0, 4, go, 0)

    def give_back(k):
        lo, hi = parts[k]
        for h in range(2):
            dx_copy(k, h).wait()
            c = slice(h * 1024, h * 1024 + 1024)
            total = dxo[lo * 8 : hi * 8, c] + dxr[lo:hi, :, c].reshape((hi - lo) * 8, 1024).astype(F32)
            rets[lo:hi, :, c] = total.astype(BF).reshape(hi - lo, 8, 1024)

            def give(i, carry):
                plane = ((z + 8 - offset(i)) % 8) * 8
                for yy in range(4):
                    e = plane + yy * 2 + h
                    src = rets.at[i * 4 + yy, :, c]

                    def send():
                        remote(src, retr.at[me], ret_s, ret_r, e, s).start()

                    if k != 1:
                        send()
                    else:
                        @pl.when(e == me)
                        def _():
                            local(src, retr.at[me], ret_r).start()

                        pl.when(e != me)(send)
                return carry

            lax.fori_loop(lo // 4, hi // 4, give, 0)

    def transpose(who, lo, hi):
        hidt[:, who * 256 + lo : who * 256 + hi] = dot(turn[...], hid[who, lo:hi, :], 1, 1).astype(BF)

    def gsum(lo, who, first_row, last_row, n):
        c = columns(n, 512)
        g = rows[1, who, first_row // 8 : last_row // 8, :, c].reshape(last_row - first_row, 512)
        return dot(hidt[lo : lo + 192, who * 256 + first_row : who * 256 + last_row], g, 1, 0)

    def early_grad(n, carry):
        gpre[:, columns(n, 512)] = gsum(192, 0, 0, 256, n) + gsum(192, 1, 0, 128, n)
        return carry

    def other_grad(n, carry):
        c = columns(n, 512)
        gsend[:, c] = (gpre[:, c] + gsum(192, 1, 128, 256, n)).astype(BF)
        return carry

    def own_grad(n, carry):
        gown[:, columns(n, 512)] = gsum(0, 0, 0, 256, n) + gsum(0, 1, 0, 256, n)
        return carry

    forward((3,))
    local(plan, planv, load_sem.at[2]).wait()
    selections()
    forward((0, 1))
    forward((2,))
    for k, src in enumerate((gw, uw, dw)):
        local(src, w.at[k, pl.ds(0, 192)], load_sem.at[3 + k]).wait()
        remote(src, w.at[k, pl.ds(192, 192)], wt_s.at[k], wt_r.at[k], me, wpart).wait()
    forward((4, 5), (2,))
    first(0, 0)
    wait_forward(0)
    first(1, 0)
    send_partial(0)
    forward((4, 5), (1, 3))
    own_partial(0)
    forward((4, 5), (0,))
    forward((6, 7), (2, 1))
    give_back(0)
    forward((6, 7), (3, 0))
    transpose(1, 0, 128)
    first(0, 1)
    transpose(0, 0, 256)
    lax.fori_loop(0, 4, early_grad, 0)
    wait_forward(1)
    kept[0], kept[1] = project(1, 1)
    transpose(1, 128, 256)

    def gp_copy(j):
        at = slice(j * 64, j * 64 + 64)
        return remote(gsend.at[at], gpart.at[at], gp_s.at[j], gp_r.at[j], me, wpart)

    lax.fori_loop(0, 4, other_grad, 0)
    for j in range(3):
        gp_copy(j).start()
    descend(1, 1, kept[0], kept[1])
    lax.fori_loop(0, 4, own_grad, 0)

    def exchange(src, dst, ss, rs, j):
        c = slice(j * 256, j * 256 + 256)

        def go(i, carry):
            plane = ((z + offset(i)) % 8) * 8
            for dy, dc in order:
                e = plane + spot[dy, dc]

                def send():
                    remote(src.at[e, :, c], dst.at[me, :, c], ss, rs.at[j], e, s).start()

                if (dy, dc) == (0, 0):
                    @pl.when(i == 3)
                    def _():
                        local(src.at[e, :, c], dst.at[me, :, c], rs.at[j]).start()

                    pl.when(i != 3)(send)
                else:
                    send()
            return carry

        lax.fori_loop(0, 8, go, 0)

    def arrived(dst, rs, j):
        got = dst.at[:, :, j * 256 : j * 256 + 256]
        local(got, got, rs.at[j]).wait()

    for j in range(3):
        gp_copy(j).wait()
        for b in range(8):
            c = slice(b * 256, (b + 1) * 256)
            at = slice(j * 64, j * 64 + 64)
            total = gown[at, c] + gpart[at, c].astype(F32)
            vst[j, b * 64 : (b + 1) * 64, :] = total.astype(BF)
        gs[:, :, j * 256 : j * 256 + 256] = dot(wv[...], vst[j], 1, 0).astype(BF).reshape(64, 8, 256)
        exchange(gs, grecv, ga_s, ga_r, j)
        if j < 2:
            send_partial(1, (j,))
        else:
            own_partial(1)

    for k, src in enumerate((mst, mom, sec)):
        local(src, states.at[k], load_sem.at[6 + k]).wait()
    for j in range(3):
        cj = slice(j * 256, j * 256 + 256)
        if j == 1:
            give_back(1)
        arrived(grecv, ga_r, j)

        def update(b, carry):
            at = pl.ds(pl.multiple_of(b * 48, 48), 48)
            c = columns(b, 256)
            f = dot(mt[at, :], grecv[:, :, cj].reshape(512, 256), 1, 0)
            m0 = states[0, j, :, c]
            nm = 0.9 * states[1, j, :, c] + 0.1 * f
            ns = 0.95 * states[2, j, :, c] + 0.05 * f * f
            first_hat = nm / (1.0 - 0.9**10)
            second_hat = ns / (1.0 - 0.95**10)
            new = m0 - 0.01 * (first_hat / (jnp.sqrt(second_hat) + 1e-08) + 0.1 * m0)
            nms[j, :, c] = new
            nmo[j, :, c] = nm
            nse[j, :, c] = ns
            nmb[at, cj] = new.astype(BF)
            return carry

        lax.fori_loop(0, 8, update, 0)
        nds[:, :, cj] = dot(mtt[...], nmb[:, cj], 1, 0).astype(BF).reshape(64, 8, 256)
        exchange(nds, ndr, nd_s, nd_r, j)

    local(retr, retr, ret_r).wait()
    for n in range(2):
        c = slice(n * 512, (n + 1) * 512)
        tgv[:, :, c] = dot(placet[...], retr[:, :, c].reshape(512, 512), 1, 0).astype(BF).reshape(2, 128, 512)
    mine = pl.ds(pl.multiple_of(core * 1024, 1024), 1024)
    tg_local = local(tgv.at[core], tg.at[:, mine], out_sem)
    tg_remote = remote(tgv.at[1 - core], tg.at[:, mine], tg_s, tg_r, other, s)
    tg_local.start()
    tg_remote.start()

    for j in range(3):
        arrived(ndr, nd_r, j)
        vst[j] = dot(wvt[...], ndr[:, :, j * 256 : j * 256 + 256].reshape(512, 256), 1, 0).astype(BF)
        for b in range(8):
            c = slice(b * 256, (b + 1) * 256)
            put = dot(back[j], vst[j, b * 64 : (b + 1) * 64, :], 1, 0)
            if j == 0:
                gpre[:, c] = put
            elif j == 1:
                gpre[:, c] += put
            else:
                ndo[:, c] = (gpre[:, c] + put).astype(BF)

    tg_local.wait()
    tg_remote.wait()
    remote(sx.at[pl.ds(0, 63)], sx.at[pl.ds(0, 63)], disp_s, disp_s, other, s).wait_send()
    remote(span(0, 0, 32), span(0, 0, 32), fwd_s, fwd_s, me, tpart).wait_send()
    remote(retr.at[pl.ds(0, 63)], retr.at[pl.ds(0, 63)], ret_s, ret_s, other, s).wait_send()
    remote(gs.at[pl.ds(0, 63)], gs.at[pl.ds(0, 63)], ga_s, ga_s, other, s).wait_send()
    remote(nds.at[pl.ds(0, 63)], nds.at[pl.ds(0, 63)], nd_s, nd_s, other, s).wait_send()


def store(*refs):
    sem = refs[-1]
    half = (len(refs) - 1) // 2
    copies = []
    for k in range(half):
        src, dst = refs[k], refs[half + k]
        for j in range(src.shape[0] if len(src.shape) == 3 else 1):
            pair = (src.at[j], dst.at[j]) if len(src.shape) == 3 else (src, dst)
            copies.append(pltpu.make_async_copy(*pair, sem.at[len(copies)]))
    for c in copies:
        c.start()
    for c in copies:
        c.wait()


def body(tokens, out_grad, routing, plan, gate_weight, up_weight, down_weight, master, moment, second):
    hbm = pl.BlockSpec(memory_space=pltpu.HBM)
    results = (
        ((128, 2048), BF),
        ((3, 48, 2048), F32),
        ((3, 48, 2048), F32),
        ((3, 48, 2048), F32),
        ((192, 2048), BF),
    )
    vm = pltpu.VMEM
    dma = pltpu.SemaphoreType.DMA
    outs = pl.pallas_call(
        kernel,
        out_shape=tuple(vm(shape, kind) for shape, kind in results),
        in_specs=[hbm] * 10,
        out_specs=[pl.BlockSpec(memory_space=pltpu.VMEM)] * 5,
        scratch_shapes=[
            vm((2, 128, 2048), BF),
            vm((2, 1, 128), jnp.int32),
            vm((1, 256), F32),
            vm((64, 8, 2048), BF),
            vm((2, 2, 32, 8, 2048), BF),
            vm((3, 384, 2048), BF),
            vm((2, 256, 384), BF),
            vm((2, 256, 384), BF),
            vm((2, 256, 384), BF),
            vm((384, 512), BF),
            vm((32, 8, 2048), BF),
            vm((32, 8, 2048), BF),
            vm((256, 2048), F32),
            vm((32, 8, 2048), BF),
            vm((64, 8, 1024), BF),
            vm((2, 128, 1024), BF),
            vm((192, 2048), BF),
            vm((192, 2048), BF),
            vm((192, 2048), F32),
            vm((3, 512, 256), BF),
            vm((64, 8, 768), BF),
            vm((64, 8, 768), BF),
            vm((1, 64), jnp.int32),
            vm((384, 512), BF),
            vm((512, 384), BF),
            vm((512, 512), BF),
            vm((512, 512), BF),
            vm((384, 384), BF),
            vm((3, 192, 64), BF),
            vm((256, 512), BF),
            vm((192, 2048), F32),
            vm((2, 128, 384), F32),
            vm((3, 3, 48, 2048), F32),
            vm((384, 768), BF),
            vm((64, 8, 768), BF),
            vm((64, 8, 768), BF),
            dma((9,)),
            dma((2,)), dma((2,)),
            dma, dma((32,)),
            dma, dma((2,)),
            dma((3,)), dma((3,)),
            dma((2, 2)), dma((2, 2)),
            dma, dma,
            dma, dma,
            dma((3,)), dma((3,)),
            dma, dma((3,)),
            dma, dma((3,)),
            dma,
        ],
        compiler_params=pltpu.CompilerParams(
            collective_id=0, has_side_effects=True, vmem_limit_bytes=58 * 1024 * 1024
        ),
    )(
        tokens,
        out_grad,
        routing.reshape(1, 128),
        plan.reshape(1, 64),
        jnp.transpose(gate_weight[0]),
        jnp.transpose(up_weight[0]),
        down_weight[0],
        jnp.transpose(master, (1, 0, 2)),
        jnp.transpose(moment, (1, 0, 2)),
        jnp.transpose(second, (1, 0, 2)),
    )
    token_grad, new_master, new_moment, new_second, new_down = pl.pallas_call(
        store,
        out_shape=tuple(jax.ShapeDtypeStruct(shape, kind) for shape, kind in results),
        in_specs=[pl.BlockSpec(memory_space=pl.ANY)] * 5,
        out_specs=[hbm] * 5,
        scratch_shapes=[dma((11,))],
        compiler_params=pltpu.CompilerParams(vmem_limit_bytes=1024 * 1024),
    )(*outs)
    back = lambda t: jnp.transpose(t, (1, 0, 2))
    return token_grad, back(new_master), back(new_moment), back(new_second), new_down[None]


def solution(mesh):
    placed = (
        P(("expert", "slot"), None),
        P(("expert", "slot"), None),
        P(("expert", "slot"), None),
        P(),
        P("expert", None, "slot"),
        P("expert", None, "slot"),
        P("expert", "slot", None),
        P(None, ("slot", "expert"), None),
        P(None, ("slot", "expert"), None),
        P(None, ("slot", "expert"), None),
    )
    return jax.shard_map(
        body,
        mesh=mesh,
        in_specs=placed,
        out_specs=(
            P(("expert", "slot"), None),
            P(None, ("slot", "expert"), None),
            P(None, ("slot", "expert"), None),
            P(None, ("slot", "expert"), None),
            P("expert", "slot", None),
        ),
        check_vma=False,
    )
```

```python
import functools

import jax
import jax.numpy as jnp
from jax import lax
from jax.experimental import pallas as pl
from jax.experimental.pallas import tpu as pltpu
from jax.sharding import PartitionSpec as P

MESH = pl.DeviceIdType.MESH
BF = jnp.bfloat16
F32 = jnp.float32


def dot(a, b, ca, cb):
    return lax.dot_general(a, b, (((ca,), (cb,)), ((), ())), preferred_element_type=F32)


def one(mask):
    return jnp.where(mask, 1.0, 0.0).astype(BF)


def iota(shape, dim):
    return lax.broadcasted_iota(jnp.int32, shape, dim)


def offset(i):
    h = i // 4
    k = i % 4
    return (1 - h) * (3 + (k * (7 - 3 * k)) // 2) + h * (4 + (2 + k // 2) * (2 * (k % 2) - 1))


def kernel(
    tok, og, route, plan, gw, uw, dw, mst, mom, sec,
    tg, nms, nmo, nse, ndo,
    dense, routes, pos, sx, rows, w, hid, dg, du, hidt,
    dxs, dxr, dxo, rets, retr, tgv,
    gsend, gpart, gown, vst, gs, grecv, planv, mt, mtt, wv, wvt, turn, back, placet, gpre, kept, states, nmb, nds, ndr,
    load_sem, swap_s, swap_r, disp_s, disp_r, fwd_s, fwd_r, wt_s, wt_r,
    dx_s, dx_r, ret_s, ret_r, tg_s, tg_r, gp_s, gp_r, ga_s, ga_r, nd_s, nd_r, out_sem,
):
    me = lax.axis_index("expert")
    s = lax.axis_index("slot")
    core = me % 2
    chip = me // 2
    z = chip // 4
    y = chip % 4
    other = me + 1 - 2 * core
    low = s + 1 - 2 * (s % 2)
    high = (s + 1 + 2 * ((s + 1) % 2)) % 4
    tpart = low + core * (high - low)
    wpart = high + core * (low - high)

    def remote(src, dst, ss, rs, e, x):
        return pltpu.make_async_remote_copy(
            src_ref=src, dst_ref=dst, send_sem=ss, recv_sem=rs, device_id=(e, x), device_id_type=MESH
        )

    def local(src, dst, sem):
        return pltpu.make_async_copy(src, dst, sem)

    barrier = pltpu.get_barrier_semaphore()

    spot = {(dy, dc): ((y + dy) % 4) * 2 + (core + dc) % 2 for dy in range(4) for dc in range(2)}
    order = [(dy, dc) for dy in (2, 1, 3, 0) for dc in (1, 0)]

    def greet(i, carry):
        plane = ((z + 4 + ((i + 1) // 2) * (1 - 2 * (i % 2)) + 8) % 8) * 8
        for dy, dc in order:
            e = plane + spot[dy, dc]
            if (dy, dc) == (0, 0):
                @pl.when(e != me)
                def _():
                    pl.semaphore_signal(barrier, inc=1, device_id=(e, s), device_id_type=MESH)
            else:
                pl.semaphore_signal(barrier, inc=1, device_id=(e, s), device_id_type=MESH)
        return carry

    lax.fori_loop(0, 8, greet, 0)
    for x in (tpart, wpart):
        pl.semaphore_signal(barrier, inc=1, device_id=(me, x), device_id_type=MESH)

    @pl.when(core == 0)
    def _():
        local(tok, dense.at[core], load_sem.at[0]).start()

    @pl.when(core == 1)
    def _():
        local(og, dense.at[core], load_sem.at[0]).start()

    local(route, routes.at[core], load_sem.at[1]).start()
    local(plan, planv, load_sem.at[2]).start()
    for k, src in enumerate((gw, uw, dw)):
        local(src, w.at[k, pl.ds(0, 192)], load_sem.at[3 + k]).start()
    for k, src in enumerate((mst, mom, sec)):
        local(src, states.at[k], load_sem.at[6 + k]).start()

    pl.semaphore_wait(barrier, 65)

    @pl.when(core == 0)
    def _():
        remote(og, dense.at[core], swap_s.at[0], swap_r.at[0], other, s).start()

    @pl.when(core == 1)
    def _():
        remote(tok, dense.at[core], swap_s.at[0], swap_r.at[0], other, s).start()

    remote(route, routes.at[core], swap_s.at[1], swap_r.at[1], other, s).start()
    for k, src in enumerate((gw, uw, dw)):
        remote(src, w.at[k, pl.ds(192, 192)], wt_s.at[k], wt_r.at[k], me, wpart).start()

    local(route, routes.at[core], load_sem.at[1]).wait()
    remote(route, routes.at[core], swap_s.at[1], swap_r.at[1], other, s).wait()
    upper = one(iota((128, 128), 0) < iota((128, 128), 1))
    for c in range(2):
        hit = iota((64, 128), 0) == routes[c]
        before = dot(one(hit), upper, 1, 0)
        rank = jnp.sum(jnp.where(hit, before, 0.0), axis=0, keepdims=True)
        pos[:, c * 128 : (c + 1) * 128] = routes[c].astype(F32) * 8.0 + (c * 4.0) + rank

    local(tok, dense.at[core], load_sem.at[0]).wait()
    remote(tok, dense.at[core], swap_s.at[0], swap_r.at[0], other, s).wait()

    def selections():
        spread = one(iota((64, 512), 0) == iota((64, 512), 1) // 8)
        held = dot(planv[...].astype(F32).astype(BF), spread, 1, 0)
        r = iota((384, 512), 0)
        m = jnp.where((r // 48 == iota((384, 512), 1) % 8) & ((r % 48).astype(F32) == held), 1.0, 0.0)
        mt[...] = m.astype(BF)
        mtt[...] = jnp.transpose(m).astype(BF)
        a = iota((512, 512), 0)
        d = iota((512, 512), 1)
        wv[...] = one((a // 8 == d % 64) & (a % 8 == d // 64))
        wvt[...] = one((d // 8 == a % 64) & (d % 8 == a // 64))
        u = iota((384, 384), 1)
        v = iota((384, 384), 0)
        turn[...] = one((u // 192 == v // 192) & (u % 192 == (v % 64) * 3 + (v % 192) // 64))
        for j in range(3):
            back[j] = one(iota((192, 64), 0) == iota((192, 64), 1) * 3 + j)
        place = jnp.where(iota((512, 256), 0).astype(F32) == pos[...], 1.0, 0.0)
        placet[...] = jnp.transpose(place).astype(BF)

    def dispatch(i, carry):
        zt = (z + offset(i)) % 8
        pick = one((iota((64, 256), 0) + zt * 64).astype(F32) == pos[...])
        block = dot(pick, dense[...].reshape(256, 2048), 1, 0).astype(BF)
        sx[pl.ds(zt * 8, 8)] = block.reshape(8, 8, 2048)
        q = i * 4 + y
        dst = rows.at[core, 0, q]
        for dy, dc in order:
            e = zt * 8 + spot[dy, dc]

            def send():
                remote(sx.at[e], dst, disp_s, disp_r.at[q], e, s).start()

            if (dy, dc) == (0, 0):
                @pl.when(i == 3)
                def _():
                    local(sx.at[e], dst, disp_r.at[q]).start()

                pl.when(i != 3)(send)
            else:
                send()
        return carry

    lax.fori_loop(0, 8, dispatch, 0)

    def span(who, q, n):
        return rows.at[:, who, pl.ds(q, n)]

    batches = ((0, 16), (16, 32))
    parts = ((0, 12), (12, 32))

    def forward(steps, dys=(2, 1, 3, 0)):
        for dy in dys:
            for i in steps:
                q = i * 4 + spot[(4 - dy) % 4, 0] // 2
                local(span(0, q, 1), span(0, q, 1), disp_r.at[q]).wait()
                remote(span(0, q, 1), span(1, q, 1), fwd_s, fwd_r.at[i // 4], me, tpart).start()

    def columns(n, size):
        return pl.ds(pl.multiple_of(n * size, size), size)

    def project(who, k):
        lo, hi = batches[k]
        x = rows[0, who, lo:hi].reshape((hi - lo) * 8, 2048)
        gate = dot(x, w[0], 1, 1)
        up = dot(x, w[1], 1, 1)
        silu = gate * jax.nn.sigmoid(gate)
        hid[who, lo * 8 : hi * 8, :] = (silu * up).astype(BF)
        return gate, up

    def descend(who, k, gate, up):
        lo, hi = batches[k]
        g = rows[1, who, lo:hi].reshape((hi - lo) * 8, 2048)
        dh = dot(g, w[2], 1, 1)
        sig = jax.nn.sigmoid(gate)
        at = slice(lo * 8, hi * 8)
        dg[who, at, :] = (dh * up * sig * (1.0 + gate * (1.0 - sig))).astype(BF)
        du[who, at, :] = (dh * (gate * sig)).astype(BF)

    def first(who, k):
        descend(who, k, *project(who, k))

    def wait_forward(k):
        lo, hi = batches[k]
        remote(span(0, lo, hi - lo), span(1, lo, hi - lo), fwd_s, fwd_r.at[k], me, tpart).wait_recv()

    def partial(who, k, n):
        lo, hi = parts[k]
        c = columns(n, 512)
        at = slice(lo * 8, hi * 8)
        return dot(dg[who, at, :], w[0, :, c], 1, 0) + dot(du[who, at, :], w[1, :, c], 1, 0)

    def dx_copy(k, h):
        lo, hi = parts[k]
        c = slice(h * 1024, h * 1024 + 1024)
        return remote(dxs.at[lo:hi, :, c], dxr.at[lo:hi, :, c], dx_s.at[k, h], dx_r.at[k, h], me, tpart)

    def send_partial(k, halves=(0, 1)):
        lo, hi = parts[k]
        for h in halves:
            def go(n, carry):
                dxs[lo:hi, :, columns(n, 512)] = partial(1, k, n).astype(BF).reshape(hi - lo, 8, 512)
                return carry

            lax.fori_loop(2 * h, 2 * h + 2, go, 0)
            dx_copy(k, h).start()

    def own_partial(k):
        lo, hi = parts[k]

        def go(n, carry):
            dxo[lo * 8 : hi * 8, columns(n, 512)] = partial(0, k, n)
            return carry

        lax.fori_loop(0, 4, go, 0)

    def give_back(k):
        lo, hi = parts[k]
        for h in range(2):
            dx_copy(k, h).wait()
            c = slice(h * 1024, h * 1024 + 1024)
            total = dxo[lo * 8 : hi * 8, c] + dxr[lo:hi, :, c].reshape((hi - lo) * 8, 1024).astype(F32)
            rets[lo:hi, :, c] = total.astype(BF).reshape(hi - lo, 8, 1024)

            def give(i, carry):
                plane = ((z + 8 - offset(i)) % 8) * 8
                for yy in range(4):
                    e = plane + yy * 2 + h
                    src = rets.at[i * 4 + yy, :, c]

                    def send():
                        remote(src, retr.at[me], ret_s, ret_r, e, s).start()

                    if k != 1:
                        send()
                    else:
                        @pl.when(e == me)
                        def _():
                            local(src, retr.at[me], ret_r).start()

                        pl.when(e != me)(send)
                return carry

            lax.fori_loop(lo // 4, hi // 4, give, 0)

    def transpose(who, lo, hi):
        hidt[:, who * 256 + lo : who * 256 + hi] = dot(turn[...], hid[who, lo:hi, :], 1, 1).astype(BF)

    def gsum(lo, who, first_row, last_row, n):
        c = columns(n, 512)
        g = rows[1, who, first_row // 8 : last_row // 8, :, c].reshape(last_row - first_row, 512)
        return dot(hidt[lo : lo + 192, who * 256 + first_row : who * 256 + last_row], g, 1, 0)

    def early_grad(n, carry):
        gpre[:, columns(n, 512)] = gsum(192, 0, 0, 256, n) + gsum(192, 1, 0, 128, n)
        return carry

    def other_grad(n, carry):
        c = columns(n, 512)
        gsend[:, c] = (gpre[:, c] + gsum(192, 1, 128, 256, n)).astype(BF)
        return carry

    def own_grad(n, carry):
        gown[:, columns(n, 512)] = gsum(0, 0, 0, 256, n) + gsum(0, 1, 0, 256, n)
        return carry

    forward((3,))
    local(plan, planv, load_sem.at[2]).wait()
    selections()
    forward((0, 1))
    forward((2,))
    for k, src in enumerate((gw, uw, dw)):
        local(src, w.at[k, pl.ds(0, 192)], load_sem.at[3 + k]).wait()
        remote(src, w.at[k, pl.ds(192, 192)], wt_s.at[k], wt_r.at[k], me, wpart).wait()
    forward((4, 5), (2,))
    first(0, 0)
    wait_forward(0)
    first(1, 0)
    send_partial(0)
    forward((4, 5), (1, 3))
    own_partial(0)
    forward((4, 5), (0,))
    forward((6, 7), (2, 1))
    give_back(0)
    forward((6, 7), (3, 0))
    transpose(1, 0, 128)
    first(0, 1)
    transpose(0, 0, 256)
    lax.fori_loop(0, 4, early_grad, 0)
    wait_forward(1)
    kept[0], kept[1] = project(1, 1)
    transpose(1, 128, 256)

    def gp_copy(j):
        at = slice(j * 64, j * 64 + 64)
        return remote(gsend.at[at], gpart.at[at], gp_s.at[j], gp_r.at[j], me, wpart)

    lax.fori_loop(0, 4, other_grad, 0)
    for j in range(3):
        gp_copy(j).start()
    descend(1, 1, kept[0], kept[1])
    lax.fori_loop(0, 4, own_grad, 0)

    def exchange(src, dst, ss, rs, j):
        c = slice(j * 256, j * 256 + 256)

        def go(i, carry):
            plane = ((z + offset(i)) % 8) * 8
            for dy, dc in order:
                e = plane + spot[dy, dc]

                def send():
                    remote(src.at[e, :, c], dst.at[me, :, c], ss, rs.at[j], e, s).start()

                if (dy, dc) == (0, 0):
                    @pl.when(i == 3)
                    def _():
                        local(src.at[e, :, c], dst.at[me, :, c], rs.at[j]).start()

                    pl.when(i != 3)(send)
                else:
                    send()
            return carry

        lax.fori_loop(0, 8, go, 0)

    def arrived(dst, rs, j):
        got = dst.at[:, :, j * 256 : j * 256 + 256]
        local(got, got, rs.at[j]).wait()

    for j in range(3):
        gp_copy(j).wait()
        for b in range(8):
            c = slice(b * 256, (b + 1) * 256)
            at = slice(j * 64, j * 64 + 64)
            total = gown[at, c] + gpart[at, c].astype(F32)
            vst[j, b * 64 : (b + 1) * 64, :] = total.astype(BF)
        gs[:, :, j * 256 : j * 256 + 256] = dot(wv[...], vst[j], 1, 0).astype(BF).reshape(64, 8, 256)
        exchange(gs, grecv, ga_s, ga_r, j)
        if j < 2:
            send_partial(1, (j,))
        else:
            own_partial(1)

    for k, src in enumerate((mst, mom, sec)):
        local(src, states.at[k], load_sem.at[6 + k]).wait()
    for j in range(3):
        cj = slice(j * 256, j * 256 + 256)
        if j == 2:
            give_back(1)
        arrived(grecv, ga_r, j)

        def update(b, carry):
            at = pl.ds(pl.multiple_of(b * 48, 48), 48)
            c = columns(b, 256)
            f = dot(mt[at, :], grecv[:, :, cj].reshape(512, 256), 1, 0)
            m0 = states[0, j, :, c]
            nm = 0.9 * states[1, j, :, c] + 0.1 * f
            ns = 0.95 * states[2, j, :, c] + 0.05 * f * f
            first_hat = nm / (1.0 - 0.9**10)
            second_hat = ns / (1.0 - 0.95**10)
            new = m0 - 0.01 * (first_hat / (jnp.sqrt(second_hat) + 1e-08) + 0.1 * m0)
            nms[j, :, c] = new
            nmo[j, :, c] = nm
            nse[j, :, c] = ns
            nmb[at, cj] = new.astype(BF)
            return carry

        lax.fori_loop(0, 8, update, 0)
        nds[:, :, cj] = dot(mtt[...], nmb[:, cj], 1, 0).astype(BF).reshape(64, 8, 256)
        exchange(nds, ndr, nd_s, nd_r, j)

    local(retr, retr, ret_r).wait()
    for n in range(2):
        c = slice(n * 512, (n + 1) * 512)
        tgv[:, :, c] = dot(placet[...], retr[:, :, c].reshape(512, 512), 1, 0).astype(BF).reshape(2, 128, 512)
    mine = pl.ds(pl.multiple_of(core * 1024, 1024), 1024)
    tg_local = local(tgv.at[core], tg.at[:, mine], out_sem)
    tg_remote = remote(tgv.at[1 - core], tg.at[:, mine], tg_s, tg_r, other, s)
    tg_local.start()
    tg_remote.start()

    for j in range(3):
        arrived(ndr, nd_r, j)
        vst[j] = dot(wvt[...], ndr[:, :, j * 256 : j * 256 + 256].reshape(512, 256), 1, 0).astype(BF)
        for b in range(8):
            c = slice(b * 256, (b + 1) * 256)
            put = dot(back[j], vst[j, b * 64 : (b + 1) * 64, :], 1, 0)
            if j == 0:
                gpre[:, c] = put
            elif j == 1:
                gpre[:, c] += put
            else:
                ndo[:, c] = (gpre[:, c] + put).astype(BF)

    tg_local.wait()
    tg_remote.wait()
    remote(sx.at[pl.ds(0, 63)], sx.at[pl.ds(0, 63)], disp_s, disp_s, other, s).wait_send()
    remote(span(0, 0, 32), span(0, 0, 32), fwd_s, fwd_s, me, tpart).wait_send()
    remote(retr.at[pl.ds(0, 63)], retr.at[pl.ds(0, 63)], ret_s, ret_s, other, s).wait_send()
    remote(gs.at[pl.ds(0, 63)], gs.at[pl.ds(0, 63)], ga_s, ga_s, other, s).wait_send()
    remote(nds.at[pl.ds(0, 63)], nds.at[pl.ds(0, 63)], nd_s, nd_s, other, s).wait_send()


def store(*refs):
    sem = refs[-1]
    half = (len(refs) - 1) // 2
    copies = []
    for k in range(half):
        src, dst = refs[k], refs[half + k]
        for j in range(src.shape[0] if len(src.shape) == 3 else 1):
            pair = (src.at[j], dst.at[j]) if len(src.shape) == 3 else (src, dst)
            copies.append(pltpu.make_async_copy(*pair, sem.at[len(copies)]))
    for c in copies:
        c.start()
    for c in copies:
        c.wait()


def body(tokens, out_grad, routing, plan, gate_weight, up_weight, down_weight, master, moment, second):
    hbm = pl.BlockSpec(memory_space=pltpu.HBM)
    results = (
        ((128, 2048), BF),
        ((3, 48, 2048), F32),
        ((3, 48, 2048), F32),
        ((3, 48, 2048), F32),
        ((192, 2048), BF),
    )
    vm = pltpu.VMEM
    dma = pltpu.SemaphoreType.DMA
    outs = pl.pallas_call(
        kernel,
        out_shape=tuple(vm(shape, kind) for shape, kind in results),
        in_specs=[hbm] * 10,
        out_specs=[pl.BlockSpec(memory_space=pltpu.VMEM)] * 5,
        scratch_shapes=[
            vm((2, 128, 2048), BF),
            vm((2, 1, 128), jnp.int32),
            vm((1, 256), F32),
            vm((64, 8, 2048), BF),
            vm((2, 2, 32, 8, 2048), BF),
            vm((3, 384, 2048), BF),
            vm((2, 256, 384), BF),
            vm((2, 256, 384), BF),
            vm((2, 256, 384), BF),
            vm((384, 512), BF),
            vm((32, 8, 2048), BF),
            vm((32, 8, 2048), BF),
            vm((256, 2048), F32),
            vm((32, 8, 2048), BF),
            vm((64, 8, 1024), BF),
            vm((2, 128, 1024), BF),
            vm((192, 2048), BF),
            vm((192, 2048), BF),
            vm((192, 2048), F32),
            vm((3, 512, 256), BF),
            vm((64, 8, 768), BF),
            vm((64, 8, 768), BF),
            vm((1, 64), jnp.int32),
            vm((384, 512), BF),
            vm((512, 384), BF),
            vm((512, 512), BF),
            vm((512, 512), BF),
            vm((384, 384), BF),
            vm((3, 192, 64), BF),
            vm((256, 512), BF),
            vm((192, 2048), F32),
            vm((2, 128, 384), F32),
            vm((3, 3, 48, 2048), F32),
            vm((384, 768), BF),
            vm((64, 8, 768), BF),
            vm((64, 8, 768), BF),
            dma((9,)),
            dma((2,)), dma((2,)),
            dma, dma((32,)),
            dma, dma((2,)),
            dma((3,)), dma((3,)),
            dma((2, 2)), dma((2, 2)),
            dma, dma,
            dma, dma,
            dma((3,)), dma((3,)),
            dma, dma((3,)),
            dma, dma((3,)),
            dma,
        ],
        compiler_params=pltpu.CompilerParams(
            collective_id=0, has_side_effects=True, vmem_limit_bytes=58 * 1024 * 1024
        ),
    )(
        tokens,
        out_grad,
        routing.reshape(1, 128),
        plan.reshape(1, 64),
        jnp.transpose(gate_weight[0]),
        jnp.transpose(up_weight[0]),
        down_weight[0],
        jnp.transpose(master, (1, 0, 2)),
        jnp.transpose(moment, (1, 0, 2)),
        jnp.transpose(second, (1, 0, 2)),
    )
    token_grad, new_master, new_moment, new_second, new_down = pl.pallas_call(
        store,
        out_shape=tuple(jax.ShapeDtypeStruct(shape, kind) for shape, kind in results),
        in_specs=[pl.BlockSpec(memory_space=pl.ANY)] * 5,
        out_specs=[hbm] * 5,
        scratch_shapes=[dma((11,))],
        compiler_params=pltpu.CompilerParams(vmem_limit_bytes=1024 * 1024),
    )(*outs)
    back = lambda t: jnp.transpose(t, (1, 0, 2))
    return token_grad, back(new_master), back(new_moment), back(new_second), new_down[None]


def solution(mesh):
    placed = (
        P(("expert", "slot"), None),
        P(("expert", "slot"), None),
        P(("expert", "slot"), None),
        P(),
        P("expert", None, "slot"),
        P("expert", None, "slot"),
        P("expert", "slot", None),
        P(None, ("slot", "expert"), None),
        P(None, ("slot", "expert"), None),
        P(None, ("slot", "expert"), None),
    )
    return jax.shard_map(
        body,
        mesh=mesh,
        in_specs=placed,
        out_specs=(
            P(("expert", "slot"), None),
            P(None, ("slot", "expert"), None),
            P(None, ("slot", "expert"), None),
            P(None, ("slot", "expert"), None),
            P("expert", "slot", None),
        ),
        check_vma=False,
    )
```
